32 devices in a mesh: tmpl: 4 (over y, core), seq: 2 (over x), tp: 4 (over z).
Axes of the slice: x: 2, y: 2, z: 4, core: 2. Of those that a mesh axis runs over, the one named last changes fastest.
Arguments:
- tokens: bfloat16 [3072, 5376], P(('tmpl', 'seq', 'tp')), parts along dimension 0, may hold values from -6 to 6
- lengths: int32 [8], P('tmpl'), parts along dimension 0, may hold values from 1 to 384, as said below
- input_gain: float32 [5376], replicated, may hold values from 0.1 to 1.9
- query_proj: bfloat16 [5376, 512], P(None, 'tp'), may hold values from -0.078125 to 0.078125
- key_value: bfloat16 [5376, 1024], P(None, 'tp'), may hold values from -0.078125 to 0.078125
- query_gain: float32 [128], replicated, may hold values from 0.5 to 20, as said below
- key_gain: float32 [128], replicated, may hold values from 0.5 to 6, as said below
- window_cache: bfloat16 [4096, 1024], P(('tmpl', 'seq'), 'tp'), parts along dimension 0, may hold values from -6 to 6
- output_proj: bfloat16 [512, 5376], P('tp', 'seq'), may hold values from -0.25 to 0.25
- post_gain: float32 [5376], replicated, may hold values from 0.1 to 1.9
Outputs:
- layer_out: bfloat16 [3072, 5376], P(('tmpl', 'seq', 'tp')), parts along dimension 0
The draws below stay inside these ranges and needn't reach their ends.
There are 4 independent parts, one for each index of `tmpl`. The reference program is written for one: setup_inputs(seed, part) draws one part's arguments, and reference() takes and returns one part's arrays. A program takes and returns all parts, laid end to end along the dimension named above; an argument that names none is the same for every part. Nothing has to cross between parts.
Inputs may be any that keep to these rules, and one draw needn't show every extreme that they name: The template's live slab tokens fill the first lengths[s] slots of seq index s, in order of s; one entry equals 384. `query_gain`: positive entries. `key_gain`: positive entries.
All inputs are finite; a program needn't handle non-finite values.
Results may differ from the reference program's by a relative error of at most 0.018.
The reference program's roundings to bfloat16 on the way (of `normed`, `queries`, `key_rows` and `head_out`) count: a program that leaves them out, or rounds other values in their place, can miss the bound.
Values may be sent and summed in bfloat16 or wider, within the bound.
A program may use at most 64 MiB of HBM per device.

```python
import math
import jax
import jax.numpy as jnp
from jax import lax

D = 5376
HD = 128
WIN = 1024
PREFIX = 32768
SLAB_DEV = 384
HEADS = 4
KV_HEADS = 4
SLOTS = 768
N_SEQ = 2


def gain_table(key, salt, low_end, high_end):
    uniform_draw = jax.random.uniform(jax.random.fold_in(key, salt), (HD,), jnp.float32)
    return jnp.exp(math.log(low_end) + uniform_draw * (math.log(high_end) - math.log(low_end)))


def draw_query_gain(key, part):
    return gain_table(key, 11, 0.5, 2.0)


def draw_key_gain(key, part):
    return gain_table(key, 12, 0.5, 2.0)


def draw_lengths(key, part):
    shard_index = jnp.arange(N_SEQ, dtype=jnp.int32)
    first_pick = jax.random.randint(jax.random.fold_in(key, 31), (N_SEQ,), 1, SLAB_DEV + 1)
    second_pick = jax.random.randint(jax.random.fold_in(key, 32), (N_SEQ,), 1, SLAB_DEV + 1)
    others = jnp.minimum(first_pick, second_pick).astype(jnp.int32)
    base_pick = jax.random.randint(jax.random.fold_in(key, 33), (), 0, SLAB_DEV - 1)
    tagged = (1 + (base_pick + part) % (SLAB_DEV - 1)).astype(jnp.int32)
    place = (jax.random.randint(jax.random.fold_in(key, 37), (), 0, N_SEQ) + part) % N_SEQ
    marked = (place + 1) % N_SEQ
    result = jnp.where(shard_index == place, SLAB_DEV, jnp.where(shard_index == marked, tagged, others))
    return result.astype(jnp.int32)


def draw_window_cache(key, part):
    cache_width = KV_HEADS * 2 * HD
    noise_draw = jnp.clip(jax.random.normal(jax.random.fold_in(key, 21), (WIN, cache_width), jnp.float32), -6.0, 6.0)
    return noise_draw.astype(jnp.bfloat16)


def shard_levels(key, shape, shards, low, top_value):
    def one(position, shards_of):
        draws = jax.random.uniform(jax.random.fold_in(jax.random.fold_in(key, 6), position), (shards_of,), jnp.float32, low / len(shards), top_value / len(shards))
        return jnp.repeat(jnp.exp(draws), shape[position] // shards_of).reshape((-1,) + (1,) * (len(shape) - position - 1))

    gain = one(*shards[0])
    for cut in shards[1:]:
        gain = gain * one(*cut)
    return gain


def scatter_about(rng, extent, width, bound, shards=(), held_as=jnp.bfloat16):
    drawn = jax.random.normal(rng, extent, jnp.float32) * width
    if len(shards) > 0:
        drawn = shard_levels(rng, extent, shards, -0.22, 0.18) * drawn
    return jnp.clip(drawn, min=-bound, max=bound).astype(held_as)


def setup_inputs(seed: int = 0, part: int = 0) -> dict:
    splits = jax.random.split(jax.random.key(seed), 11)
    part_keys = jax.random.split(jax.random.fold_in(splits[10], part), 11)
    return {
        "tokens": scatter_about(part_keys[0], (SLOTS, D), 1.0, 6.0, ((0, 8),)),
        "lengths": draw_lengths(jax.random.fold_in(jax.random.fold_in(splits[10], part), 71), part),
        "input_gain": jnp.clip(1.0 + 0.18 * jax.random.normal(splits[2], (D,), jnp.float32), 0.1, 1.9),
        "query_proj": scatter_about(splits[3], (D, HEADS * HD), D ** -0.5, 0.078125, ((1, 4),)),
        "key_value": scatter_about(splits[4], (D, KV_HEADS * 2 * HD), D ** -0.5, 0.078125, ((1, 4),)),
        "query_gain": draw_query_gain(jax.random.fold_in(splits[10], 71), part),
        "key_gain": draw_key_gain(jax.random.fold_in(splits[10], 71), part),
        "window_cache": draw_window_cache(jax.random.fold_in(jax.random.fold_in(splits[10], part), 71), part),
        "output_proj": scatter_about(splits[8], (HEADS * HD, D), (HEADS * HD) ** -0.5, 0.25, ((0, 4), (1, 2))),
        "post_gain": jnp.clip(1.0 + 0.18 * jax.random.normal(splits[9], (D,), jnp.float32), 0.1, 1.9),
    }


EPSILON = 1e-06
ROPE_BASE = 10000.0
QUERY_SCALE = 168.0 ** (-0.5)
MASKED = -1e+30

def normalize(values, scale_gain):
    values = values.astype(jnp.float32)
    return values * lax.rsqrt(lax.optimization_barrier(jnp.mean(values * values, axis=-1, keepdims=True)) + EPSILON) * scale_gain

def rotate(values, positions):
    half_width = values.shape[-1] // 2
    frequency = jnp.power(ROPE_BASE, -2.0 * jnp.arange(half_width, dtype=jnp.float32) / values.shape[-1])
    angles = positions.astype(jnp.float32)[:, None] * frequency[None, :]
    cosine_table = jnp.cos(angles)
    sine_table = jnp.sin(angles)
    first_half = values[:, :half_width]
    second_half = values[:, half_width:]
    return jnp.concatenate([first_half * cosine_table - second_half * sine_table, second_half * cosine_table + first_half * sine_table], axis=1)

def reference(tokens, lengths, input_gain, query_proj, key_value, query_gain, key_gain, window_cache, output_proj, post_gain):
    normed = normalize(tokens, input_gain).astype(jnp.bfloat16)
    query_raw = jnp.dot(normed, query_proj, preferred_element_type=jnp.float32)
    kv_raw = jnp.dot(normed, key_value, preferred_element_type=jnp.float32)
    offsets = (jnp.cumsum(lengths) - lengths).astype(jnp.int32)
    slot_index = jnp.arange(SLAB_DEV, dtype=jnp.int32)
    positions = (PREFIX + offsets[:, None] + slot_index[None, :]).reshape(-1).astype(jnp.int32)
    live_rows = (slot_index[None, :] < lengths[:, None]).reshape(-1)
    cache_position = (PREFIX - WIN + jnp.arange(WIN, dtype=jnp.int32)).astype(jnp.int32)
    key_position = jnp.concatenate([cache_position, positions])
    key_live = jnp.concatenate([jnp.ones((WIN,), dtype=bool), live_rows])
    allowed = key_live[None, :] & (key_position[None, :] <= positions[:, None]) & (key_position[None, :] > positions[:, None] - WIN)
    projection = jnp.zeros((tokens.shape[0], tokens.shape[1]), jnp.float32)
    for head_index in range(HEADS):
        queries = (rotate(normalize(query_raw[:, head_index * HD:(head_index + 1) * HD], query_gain), positions) * QUERY_SCALE).astype(jnp.bfloat16)
        new_keys = rotate(normalize(kv_raw[:, 2 * head_index * HD:(2 * head_index + 1) * HD], key_gain), positions).astype(jnp.bfloat16)
        new_values = kv_raw[:, (2 * head_index + 1) * HD:(2 * head_index + 2) * HD].astype(jnp.bfloat16)
        key_rows = jnp.concatenate([window_cache[:, 2 * head_index * HD:(2 * head_index + 1) * HD], new_keys], axis=0)
        value_rows = jnp.concatenate([window_cache[:, (2 * head_index + 1) * HD:(2 * head_index + 2) * HD], new_values], axis=0)
        scores = jnp.dot(queries, key_rows.T, preferred_element_type=jnp.float32)
        scores = jnp.where(allowed, scores, MASKED)
        row_max = lax.optimization_barrier(jnp.max(scores, axis=1, keepdims=True))
        weights = jnp.where(allowed, jnp.exp(scores - row_max), 0.0)
        row_sum = lax.optimization_barrier(jnp.sum(weights, axis=1))
        head_out = jnp.dot(weights.astype(jnp.bfloat16), value_rows, preferred_element_type=jnp.float32)
        head_out = head_out / jnp.where(live_rows, row_sum, 1.0)[:, None]
        head_out = jnp.where(live_rows[:, None], head_out, 0.0).astype(jnp.bfloat16)
        head_term = jnp.dot(head_out, output_proj[head_index * HD:(head_index + 1) * HD], preferred_element_type=jnp.float32).astype(jnp.bfloat16)
        projection = projection + lax.optimization_barrier(head_term).astype(jnp.float32)
    post_norm = normalize(projection, post_gain)
    return (tokens.astype(jnp.float32) + post_norm).astype(jnp.bfloat16)
```

```python
import functools

import jax
import jax.numpy as jnp
import numpy as np
from jax import lax
from jax.experimental import pallas as pl
from jax.experimental.pallas import tpu as pltpu
from jax.sharding import PartitionSpec as P

WIN = 1024
PREFIX = 32768
EPSILON = 1e-06
ROPE_BASE = 10000.0
QUERY_SCALE = 168.0 ** (-0.5)
MASKED = -1e30
F32 = jnp.float32
BF16 = jnp.bfloat16
MESH = pl.DeviceIdType.MESH


def chunk_of(width, limit):
    best = 128
    for c in range(128, limit + 1, 128):
        if width % c == 0:
            best = c
    return best


def flat(v):
    shape = (v.shape[0] * v.shape[1], v.shape[2])
    if v.shape[1] % 16 == 0:
        return v.reshape(shape)
    return v.astype(F32).reshape(shape).astype(v.dtype)


def kernel(
    T, S, N, S2, NC, RC,
    lengths, tokens, wq_hbm, wkv_hbm, cache_hbm, oproj_hbm,
    ig_hbm, pg_hbm, qgain, kgain, freq,
    out_ref,
    igs, pgs, igain, pgain, cos_t, sin_t, xbuf, nbuf, w, cbuf, og, q_all, kv_all, q_snd, kv_snd, hsnd, ho, proj,
    lsem, s_w, s_x, s_c, s_o, s_oz, s_kvx, s_kv, s_q, s_h,
    r_x, r_c, r_own, r_w, r_o, r_q, r_kv, r_kvx, r_h,
):
    t, s, z = lax.axis_index("tmpl"), lax.axis_index("seq"), lax.axis_index("tp")
    h = N // 2
    p, b = z // h, z % h
    op = 1 - p
    zp = (z + h) % N
    R, D = tokens.shape
    HW = wq_hbm.shape[1]
    C = cache_hbm.shape[0]
    DE = D // (T * S2)
    DN = DE // NC
    RR = R // RC
    OR = oproj_hbm.shape[0] // T
    DC = oproj_hbm.shape[1]
    tc = t + 1 - 2 * (t % 2)
    par = t % 2
    ys = [(t + 2 * k) % T for k in range(1, T // 2)]
    same = [t] + ys
    cross = [(tc + 2 * k) % T for k in range(T // 2)]
    xs = [(s + k) % S for k in range(1, S)]
    sg, sb = (s // S2) * S2, s % S2
    x2 = [(sb + k) % S2 for k in range(1, S2)]
    zs = [(z + k) % N for k in range(1, N)]

    def copy(src, dst, ssem, rsem, dev):
        return pltpu.make_async_remote_copy(
            src_ref=src, dst_ref=dst, send_sem=ssem, recv_sem=rsem,
            device_id=dev, device_id_type=MESH,
        )

    def send(src, dst, ssem, rsem, dev):
        copy(src, dst, ssem, rsem, dev).start()

    def arrived(dst, rsem):
        copy(dst, dst, s_q, rsem, {"tp": zp}).wait_recv()

    def left(src, ssem):
        copy(src, src, ssem, r_q, {"tp": zp}).wait_send()

    loc = [
        pltpu.make_async_copy(tokens, xbuf.at[b], lsem.at[0]),
        pltpu.make_async_copy(wq_hbm, w.at[0, :, pl.ds(0, HW)], lsem.at[1]),
        pltpu.make_async_copy(wkv_hbm, w.at[0, :, pl.ds(HW, 2 * HW)], lsem.at[2]),
        pltpu.make_async_copy(ig_hbm, igs, lsem.at[3]),
        pltpu.make_async_copy(pg_hbm, pgs, lsem.at[4]),
        pltpu.make_async_copy(cache_hbm, cbuf.at[s], lsem.at[5]),
    ]

    def slab(ks, kt, n):
        return (ks * T + kt) * N + n

    for k in range(T):
        loc.append(
            pltpu.make_async_copy(
                oproj_hbm.at[pl.ds(k * OR, OR)], og.at[slab(s, k, z)], lsem.at[6 + k]
            )
        )
    for c in loc:
        c.start()

    barrier = pltpu.get_barrier_semaphore()
    peers = (
        [{"tp": k} for k in zs] + [{"seq": k} for k in xs]
        + [{"tmpl": k} for k in ys] + [{"tmpl": tc}]
    )
    for dev in peers:
        pl.semaphore_signal(barrier, inc=1, device_id=dev, device_id_type=MESH)
    pl.semaphore_wait(barrier, len(peers))

    def piece(e_t, e_s, c):
        return pl.ds(pl.multiple_of((e_t * S2 + e_s) * DE + c * DN, DN), DN)

    loc[1].wait()
    loc[2].wait()

    def send_w():
        for c in range(NC):
            pc = piece(t, sb, c)
            send(w.at[0, pc], w.at[1, pc], s_w, r_own.at[c], {"tp": zp})

    def send_rows(c):
        rows = pl.ds(c * RR, RR)
        for k in range(1, h):
            send(tokens.at[rows], xbuf.at[b, rows], s_x, r_x.at[b, c], {"tp": p * h + (b + k) % h})

    @pl.when(par == 0)
    def _():
        send_w()
        for c in range(RC):
            send_rows(c)

    @pl.when(par == 1)
    def _():
        send_rows(0)
        send_w()
        for c in range(1, RC):
            send_rows(c)

    for k in xs:
        send(cache_hbm, cbuf.at[s], s_c, r_c.at[s], {"seq": k})

    lens = [lengths[k] for k in range(S)]
    offs = []
    total = jnp.int32(0)
    for k in range(S):
        offs.append(total)
        total = total + lens[k]
    own_off = jnp.int32(0)
    own_len = jnp.int32(0)
    for k in range(S):
        own_off = own_off + jnp.where(s == k, offs[k], 0)
        own_len = own_len + jnp.where(s == k, lens[k], 0)

    RB = 16 if RR % 16 == 0 else 8
    KC = chunk_of(D, 1024)

    def norm_rows(slot, first, count):
        def body(i, carry):
            rows = pl.ds(pl.multiple_of(first + i * RB, RB), RB)
            v = xbuf[slot, rows, :].astype(F32)
            inv = lax.rsqrt(jnp.sum(v * v, axis=1, keepdims=True) * (1.0 / D) + EPSILON)
            nbuf[slot, rows, :] = (v * inv * igain[...]).astype(BF16)
            return carry

        lax.fori_loop(0, count // RB, body, 0)

    def head_norm(v, gain):
        inv = lax.rsqrt(jnp.mean(v * v, axis=1, keepdims=True) + EPSILON)
        return v * inv * gain

    def project(slot, j):
        def body(i, acc):
            ks = pl.ds(pl.multiple_of(i * KC, KC), KC)
            return acc + jnp.dot(nbuf[slot, :, ks], w[j, ks, :], preferred_element_type=F32)

        v = lax.fori_loop(0, D // KC, body, jnp.zeros((R, 3 * HW), F32))
        co, si = cos_t[slot], sin_t[slot]

        def rope(u):
            return u * co + pltpu.roll(u, HW // 2, 1) * si

        q = (rope(head_norm(v[:, :HW], qgain[...])) * QUERY_SCALE).astype(BF16)
        k = rope(head_norm(v[:, HW : 2 * HW], kgain[...])).astype(BF16)
        return q, jnp.concatenate([k, v[:, 2 * HW :].astype(BF16)], axis=1)

    def share(n):
        for k in xs:
            send(kv_all.at[s, n], kv_all.at[s, n], s_kvx, r_kvx.at[s], {"seq": k})

    def own_head(slot):
        q, kv = project(slot, 0)
        n = p * h + slot
        q_all[n] = q
        kv_all[s, n] = kv
        share(n)

    def other_head(slot):
        q, kv = project(slot, 1)
        n = p * h + slot
        q_snd[slot] = q
        kv_snd[slot] = kv
        send(kv_snd.at[slot], kv_all.at[s, n], s_kv, r_kv, {"tp": zp})
        send(q_snd.at[slot], q_all.at[n], s_q, r_q, {"tp": zp})

    loc[3].wait()
    loc[4].wait()
    for k in range(D // 128):
        igain[0:1, k * 128 : (k + 1) * 128] = igs[k : k + 1, :]
        pgain[0:1, k * 128 : (k + 1) * 128] = pgs[k : k + 1, :]
    lane = lax.broadcasted_iota(jnp.int32, (R, HW), 1)
    for k in range(h):
        row = lax.broadcasted_iota(jnp.int32, (R, HW), 0)
        angle = (PREFIX + own_off + (p * h + k) * R + row).astype(F32) * freq[...]
        cos_t[k] = jnp.cos(angle)
        sine = jnp.sin(angle)
        sin_t[k] = jnp.where(lane < HW // 2, -sine, sine)
    loc[0].wait()
    norm_rows(b, 0, R)
    own_head(b)
    for k in range(T):
        loc[6 + k].wait()

    def o_copy(idx, dev, ssem=None):
        send(og.at[idx], og.at[idx], s_o if ssem is None else ssem, r_o.at[idx], dev)

    def z_right(n):
        @pl.when(z < N - 1)
        def _():
            o_copy(slab(s, t, n), {"tp": jnp.minimum(z + 1, N - 1)}, s_oz.at[n])

    def z_left(n):
        @pl.when(z > 0)
        def _():
            o_copy(slab(s, t, n), {"tp": jnp.maximum(z - 1, 0)}, s_oz.at[N + n])

    def o_arrive(d):
        @pl.when(z + d < N)
        def _():
            n = z + d
            arrived(og.at[slab(s, t, n)], r_o.at[slab(s, t, n)])
            z_left(n)
            o_plane(n)

        @pl.when(z - d >= 0)
        def _():
            n = z - d
            arrived(og.at[slab(s, t, n)], r_o.at[slab(s, t, n)])
            z_right(n)
            o_plane(n)

    def o_plane(n):
        i = slab(s, t, n)
        for k in xs:
            o_copy(i, {"seq": k})
        for k in ys:
            o_copy(i, {"tmpl": k})
        o_copy(i, {"tmpl": tc})

    def each(d, fn):
        @pl.when(z + d < N)
        def _():
            fn(z + d)

        @pl.when(z - d >= 0)
        def _():
            fn(z - d)

    def o_x(n):
        for ks in xs:
            i = slab(ks, t, n)
            arrived(og.at[i], r_o.at[i])
            for k in ys:
                o_copy(i, {"tmpl": k})
            o_copy(i, {"tmpl": tc})

    def o_y(n):
        for kt in ys:
            for ks in [s] + xs:
                i = slab(ks, kt, n)
                arrived(og.at[i], r_o.at[i])
                o_copy(i, {"tmpl": tc})

    def o_last(n):
        for kt in cross:
            for ks in [s] + xs:
                i = slab(ks, kt, n)
                arrived(og.at[i], r_o.at[i])

    def own_x():
        for kt in same:
            for k in xs:
                o_copy(slab(s, kt, z), {"seq": k})

    def own_c():
        for ks in xs:
            for kt in same:
                i = slab(ks, kt, z)
                arrived(og.at[i], r_o.at[i])
                o_copy(i, {"tmpl": tc})

    def own_last():
        for ks in xs:
            for kt in cross:
                i = slab(ks, kt, z)
                arrived(og.at[i], r_o.at[i])

    z_right(z)
    z_left(z)

    def w_own(c):
        pc = piece(t, sb, c)
        arrived(w.at[1, pc], r_own.at[c])
        for k in x2:
            send(w.at[1, pc], w.at[1, pc], s_w, r_w.at[t, sb, c], {"seq": sg + k})
        for k in ys:
            send(w.at[1, pc], w.at[1, pc], s_w, r_w.at[t, sb, c], {"tmpl": k})
        send(w.at[1, pc], w.at[1, pc], s_w, r_w.at[t, sb, c], {"tmpl": tc})

    def w_x(c):
        for k2 in x2:
            pc = piece(t, k2, c)
            arrived(w.at[1, pc], r_w.at[t, k2, c])
            for k in ys:
                send(w.at[1, pc], w.at[1, pc], s_w, r_w.at[t, k2, c], {"tmpl": k})
            send(w.at[1, pc], w.at[1, pc], s_w, r_w.at[t, k2, c], {"tmpl": tc})

    def w_y(c):
        for k in ys:
            for ks in range(S2):
                pc = piece(k, ks, c)
                arrived(w.at[1, pc], r_w.at[k, ks, c])
                send(w.at[1, pc], w.at[1, pc], s_w, r_w.at[k, ks, c], {"tmpl": tc})

    for i in range(NC + 1):
        if i < NC:
            w_own(i)
        if i > 0:
            w_x(i - 1)
    own_x()
    for c in range(NC):
        w_y(c)
    for c in range(NC):
        for kt in cross:
            for ks in range(S2):
                arrived(w.at[1, piece(kt, ks, c)], r_w.at[kt, ks, c])
    other_head(b)
    for k in range(1, h):
        slot = (b + k) % h
        for c in range(RC):
            rows = pl.ds(c * RR, RR)
            arrived(xbuf.at[slot, rows], r_x.at[slot, c])
            norm_rows(slot, c * RR, RR)
        other_head(slot)
    for k in range(1, h):
        own_head((b + k) % h)

    own_c()
    o_arrive(1)
    arrived(kv_all.at[s, pl.ds(op * h, h)], r_kv)
    for i in range(h):
        share(op * h + i)
    arrived(q_all.at[pl.ds(op * h, h)], r_q)
    each(1, o_x)
    loc[5].wait()
    for k in xs:
        arrived(cbuf.at[k], r_c.at[k])
        arrived(kv_all.at[k], r_kvx.at[k])

    def attend(d, carry):
        n = lax.rem(z + d, N)
        q = q_all[n]
        slot_c = n * R + lax.broadcasted_iota(jnp.int32, (R, 1), 0)
        pos = PREFIX + own_off + slot_c
        scores, allow, values = [], [], []
        for k in range(S):
            cb = cbuf[k]
            sc = lax.dot_general(
                q, cb[:, :HW], (((1,), (1,)), ((), ())), preferred_element_type=F32
            )
            kp = PREFIX - WIN + k * C + lax.broadcasted_iota(jnp.int32, (1, C), 1)
            ok = (kp <= pos) & (kp > pos - WIN)
            scores.append(jnp.where(ok, sc, MASKED))
            allow.append(ok)
            values.append(cb[:, HW:])
            kv = flat(kv_all[k])
            sc = lax.dot_general(
                q, kv[:, :HW], (((1,), (1,)), ((), ())), preferred_element_type=F32
            )
            j = lax.broadcasted_iota(jnp.int32, (1, N * R), 1)
            kp = PREFIX + offs[k] + j
            ok = (kp <= pos) & (kp > pos - WIN) & (j < lens[k])
            scores.append(jnp.where(ok, sc, MASKED))
            allow.append(ok)
            values.append(kv[:, HW:])
        top = functools.reduce(
            jnp.maximum, [jnp.max(v, axis=1, keepdims=True) for v in scores]
        )
        row_sum = jnp.zeros((R, 1), F32)
        acc = jnp.zeros((R, HW), F32)
        for sc, ok, vv in zip(scores, allow, values):
            wt = jnp.where(ok, jnp.exp(sc - top), 0.0)
            row_sum = row_sum + jnp.sum(wt, axis=1, keepdims=True)
            acc = acc + jnp.dot(wt.astype(BF16), vv, preferred_element_type=F32)
        live = slot_c < own_len
        res = acc / jnp.where(live, row_sum, 1.0)
        hsnd[n] = jnp.where(live, res, 0.0).astype(BF16)

        @pl.when(d < N)
        def _():
            send(hsnd.at[n], ho.at[z], s_h, r_h, {"tp": n})

        return carry

    lax.fori_loop(1, N + 1, attend, 0)
    ho[z] = hsnd[z]

    for d in range(2, N):
        o_arrive(d)
        each(d - 1, o_y)
        each(d, o_x)
    each(N - 1, o_y)
    own_last()
    for d in range(1, N):
        each(d, o_last)
    arrived(ho.at[pl.ds(0, N - 1)], r_h)

    CC = chunk_of(DC, 1024)

    for k in range(S):
        def cols(i, carry):
            cs = pl.ds(pl.multiple_of(i * CC, CC), CC)
            acc = jnp.zeros((R, CC), F32)
            for g in range(N):
                wt = jnp.concatenate([og[slab(k, kt, g), :, cs] for kt in range(T)], axis=0)
                acc = acc + jnp.dot(ho[g], wt, preferred_element_type=F32).astype(BF16).astype(F32)
            proj[:, pl.ds(pl.multiple_of(k * DC + i * CC, 128), CC)] = acc
            return carry

        lax.fori_loop(0, DC // CC, cols, 0)

    RF = 16 if R % 16 == 0 else 8

    def finish(i, carry):
        rows = pl.ds(pl.multiple_of(i * RF, RF), RF)
        v = proj[rows, :]
        inv = lax.rsqrt(jnp.sum(v * v, axis=1, keepdims=True) * (1.0 / D) + EPSILON)
        out_ref[rows, :] = (xbuf[b, rows, :].astype(F32) + v * inv * pgain[...]).astype(BF16)
        return carry

    lax.fori_loop(0, R // RF, finish, 0)

    left(w.at[1], s_w)
    left(xbuf.at[pl.ds(0, h - 1)], s_x)
    left(cbuf.at[pl.ds(0, S - 1)], s_c)
    left(kv_all.at[pl.ds(0, S - 1)], s_kvx)
    left(kv_snd, s_kv)
    left(q_snd, s_q)
    left(hsnd.at[pl.ds(0, N - 1)], s_h)
    X, Y = S - 1, T // 2 - 1
    count = (N - 1) * (X + Y + 1 + X * (Y + 1) + Y * S) + (Y + 1) * X * 2
    while count > 0:
        part = min(count, S * T * N)
        left(og.at[pl.ds(0, part)], s_o)
        count -= part
    for n in range(N):
        @pl.when((n <= z) & (z < N - 1))
        def _():
            left(og.at[0], s_oz.at[n])

        @pl.when((n >= z) & (z > 0))
        def _():
            left(og.at[0], s_oz.at[N + n])


def shards(
    T, S, N,
    tokens, lengths, input_gain, query_proj, key_value, query_gain, key_gain,
    window_cache, output_proj, post_gain,
):
    R, D = tokens.shape
    HW = query_proj.shape[1]
    C = window_cache.shape[0]
    h = N // 2
    S2 = max(d for d in range(1, S + 1) if S % d == 0 and D % (16 * T * d) == 0)
    NC = max(d for d in (1, 2, 3) if D // (T * S2) % (16 * d) == 0)
    RC = 3 if R % 48 == 0 else 1
    inv = np.power(ROPE_BASE, -2.0 * np.arange(HW // 2) / HW)
    freq = np.concatenate([inv, inv])[None, :].astype(np.float32)
    OR, DC = output_proj.shape[0] // T, output_proj.shape[1]
    vm = pl.BlockSpec(memory_space=pltpu.VMEM)
    hb = pl.BlockSpec(memory_space=pltpu.HBM)
    dma = pltpu.SemaphoreType.DMA
    return pl.pallas_call(
        functools.partial(kernel, T, S, N, S2, NC, RC),
        out_shape=jax.ShapeDtypeStruct((R, D), BF16),
        in_specs=[pl.BlockSpec(memory_space=pltpu.SMEM), hb, hb, hb, hb, hb]
        + [hb, hb, vm, vm, vm],
        out_specs=vm,
        scratch_shapes=[
            pltpu.VMEM((D // 128, 128), F32),
            pltpu.VMEM((D // 128, 128), F32),
            pltpu.VMEM((1, D), F32),
            pltpu.VMEM((1, D), F32),
            pltpu.VMEM((h, R, HW), F32),
            pltpu.VMEM((h, R, HW), F32),
            pltpu.VMEM((h, R, D), BF16),
            pltpu.VMEM((h, R, D), BF16),
            pltpu.VMEM((2, D, 3 * HW), BF16),
            pltpu.VMEM((S, C, 2 * HW), BF16),
            pltpu.VMEM((S * T * N, OR, DC), BF16),
            pltpu.VMEM((N, R, HW), BF16),
            pltpu.VMEM((S, N, R, 2 * HW), BF16),
            pltpu.VMEM((h, R, HW), BF16),
            pltpu.VMEM((h, R, 2 * HW), BF16),
            pltpu.VMEM((N, R, HW), BF16),
            pltpu.VMEM((N, R, HW), BF16),
            pltpu.VMEM((R, D), F32),
            dma((6 + T,)), dma, dma, dma, dma, dma((2 * N,)), dma, dma, dma, dma,
            dma((h, RC)), dma((S,)), dma((NC,)), dma((T, S2, NC)), dma((S * T * N,)),
            dma, dma, dma((S,)), dma,
        ],
        compiler_params=pltpu.CompilerParams(
            collective_id=0, has_side_effects=True, vmem_limit_bytes=67043328 - 2 * R * D * 2
        ),
    )(
        lengths, tokens, query_proj, key_value, window_cache, output_proj,
        input_gain.reshape(D // 128, 128), post_gain.reshape(D // 128, 128),
        query_gain[None, :], key_gain[None, :], jnp.asarray(freq),
    )


def solution(mesh):
    T, S, N = mesh.shape["tmpl"], mesh.shape["seq"], mesh.shape["tp"]
    return jax.shard_map(
        functools.partial(shards, T, S, N),
        mesh=mesh,
        in_specs=(
            P(("tmpl", "seq", "tp"), None),
            P("tmpl"),
            P(),
            P(None, "tp"),
            P(None, "tp"),
            P(),
            P(),
            P(("tmpl", "seq"), "tp"),
            P("tp", "seq"),
            P(),
        ),
        out_specs=P(("tmpl", "seq", "tp"), None),
        check_vma=False,
    )
```

```python
import functools

import jax
import jax.numpy as jnp
import numpy as np
from jax import lax
from jax.experimental import pallas as pl
from jax.experimental.pallas import tpu as pltpu
from jax.sharding import PartitionSpec as P

WIN = 1024
PREFIX = 32768
EPSILON = 1e-06
ROPE_BASE = 10000.0
QUERY_SCALE = 168.0 ** (-0.5)
MASKED = -1e30
F32 = jnp.float32
BF16 = jnp.bfloat16
MESH = pl.DeviceIdType.MESH


VIA_X = ()
PLANS = {
    (0, False): (
        "SW", "Z1", "Z2", "R0", "R1", "R2", "Z3", "SO", "OWN", "W0", "W1", "A0",
        "W2", "A1", "B0", "W3", "A2", "B1", "W4", "A3", "B2", "XZ", "W5", "A4",
        "B3", "A5", "B4", "P1", "B5", "P2", "SC", "WC", "OB", "X1", "RN", "ON",
        "KE", "X2", "Y1", "KV", "P3", "KX", "AT", "X3", "D1", "DZ", "Y2", "D2",
        "Y3", "D3",
    ),
    (0, True): (
        "SW", "R0", "R1", "R2", "Z1", "Z2", "Z3", "SO", "OWN", "W0", "W1", "A0",
        "W2", "A1", "B0", "W3", "A2", "B1", "W4", "A3", "B2", "XZ", "W5", "A4",
        "B3", "A5", "B4", "P1", "B5", "P2", "SC", "WC", "OB", "X1", "RN", "ON",
        "KE", "X2", "Y1", "KV", "P3", "KX", "AT", "X3", "D1", "DZ", "Y2", "D2",
        "Y3", "D3",
    ),
    (1, False): (
        "R0", "SW", "Z1", "R1", "R2", "Z2", "Z3", "SO", "OWN", "W0", "W1", "A0",
        "W2", "A1", "B0", "W3", "A2", "B1", "W4", "A3", "B2", "XZ", "W5", "A4",
        "B3", "A5", "B4", "P1", "B5", "P2", "SC", "WC", "OB", "X1", "RN", "ON",
        "KE", "X2", "Y1", "KV", "P3", "KX", "AT", "X3", "D1", "DZ", "Y2", "D2",
        "Y3", "D3",
    ),
    (1, True): (
        "SW", "SO", "OWN", "W0", "W1", "A0", "W2", "A1", "B0", "W3", "A2", "B1",
        "W4", "A3", "B2", "XZ", "W5", "A4", "B3", "Z1", "R0", "R1", "R2", "Z2",
        "Z3", "A5", "B4", "P1", "B5", "P2", "SC", "WC", "OB", "X1", "RN", "ON",
        "KE", "X2", "Y1", "KV", "P3", "KX", "AT", "X3", "D1", "DZ", "Y2", "D2",
        "Y3", "D3",
    ),
}


def chunk_of(width, limit):
    best = 128
    for c in range(128, limit + 1, 128):
        if width % c == 0:
            best = c
    return best


def flat(v):
    shape = (v.shape[0] * v.shape[1], v.shape[2])
    if v.shape[1] % 16 == 0:
        return v.reshape(shape)
    return v.astype(F32).reshape(shape).astype(v.dtype)


def kernel(
    T, S, N, S2, NC, RC,
    lengths, tokens, wq_hbm, wkv_hbm, cache_hbm, oproj_hbm,
    ig_hbm, pg_hbm, qgain, kgain, freq,
    out_ref,
    igs, pgs, igain, pgain, cos_t, sin_t, xbuf, nbuf, w, cbuf, og, q_all, kv_all, q_snd, kv_snd, hsnd, ho, proj, obuf,
    lsem, osem, s_w, s_x, s_c, s_o, s_oz, s_kvx, s_kv, s_q, s_h,
    r_x, r_c, r_own, r_w, r_o, r_q, r_kv, r_kvx, r_h,
):
    t, s, z = lax.axis_index("tmpl"), lax.axis_index("seq"), lax.axis_index("tp")
    h = N // 2
    p, b = z // h, z % h
    op = 1 - p
    zp = (z + h) % N
    R, D = tokens.shape
    HW = wq_hbm.shape[1]
    C = cache_hbm.shape[0]
    DE = D // (T * S2)
    DN = DE // NC
    RR = R // RC
    OR = oproj_hbm.shape[0] // T
    DC = oproj_hbm.shape[1]
    tc = t + 1 - 2 * (t % 2)
    par = t % 2
    ys = [(t + 2 * k) % T for k in range(1, T // 2)]
    same = [t] + ys
    cross = [(tc + 2 * k) % T for k in range(T // 2)]
    xs = [(s + k) % S for k in range(1, S)]
    sg, sb = (s // S2) * S2, s % S2
    x2 = [(sb + k) % S2 for k in range(1, S2)]
    zs = [(z + k) % N for k in range(1, N)]

    def copy(src, dst, ssem, rsem, dev):
        return pltpu.make_async_remote_copy(
            src_ref=src, dst_ref=dst, send_sem=ssem, recv_sem=rsem,
            device_id=dev, device_id_type=MESH,
        )

    def send(src, dst, ssem, rsem, dev):
        copy(src, dst, ssem, rsem, dev).start()

    def arrived(dst, rsem):
        copy(dst, dst, s_q, rsem, {"tp": zp}).wait_recv()

    def left(src, ssem):
        copy(src, src, ssem, r_q, {"tp": zp}).wait_send()

    loc = [
        pltpu.make_async_copy(tokens, xbuf.at[b], lsem.at[0]),
        pltpu.make_async_copy(wq_hbm, w.at[0, :, pl.ds(0, HW)], lsem.at[1]),
        pltpu.make_async_copy(wkv_hbm, w.at[0, :, pl.ds(HW, 2 * HW)], lsem.at[2]),
        pltpu.make_async_copy(ig_hbm, igs, lsem.at[3]),
        pltpu.make_async_copy(pg_hbm, pgs, lsem.at[4]),
        pltpu.make_async_copy(cache_hbm, cbuf.at[s], lsem.at[5]),
    ]

    def slab(ks, kt, n):
        return (ks * T + kt) * N + n

    for k in range(T):
        loc.append(
            pltpu.make_async_copy(
                oproj_hbm.at[pl.ds(k * OR, OR)], og.at[slab(s, k, z)], lsem.at[6 + k]
            )
        )
    for c in loc:
        c.start()

    barrier = pltpu.get_barrier_semaphore()
    peers = (
        [{"tp": k} for k in zs] + [{"seq": k} for k in xs]
        + [{"tmpl": k} for k in ys] + [{"tmpl": tc}]
    )
    for dev in peers:
        pl.semaphore_signal(barrier, inc=1, device_id=dev, device_id_type=MESH)
    pl.semaphore_wait(barrier, len(peers))

    def piece(e_t, e_s, c):
        return pl.ds(pl.multiple_of((e_t * S2 + e_s) * DE + c * DN, DN), DN)

    def send_w():
        for c in range(NC):
            pc = piece(t, sb, c)
            for src, at in ((wq_hbm, pl.ds(0, HW)), (wkv_hbm, pl.ds(HW, 2 * HW))):
                send(src.at[pc], w.at[1, pc, at], s_w, r_own.at[c], {"tp": zp})

    def send_rows(c):
        rows = pl.ds(c * RR, RR)
        for k in range(1, h):
            send(tokens.at[rows], xbuf.at[b, rows], s_x, r_x.at[b, c], {"tp": p * h + (b + k) % h})

    def o_copy(idx, dev):
        send(og.at[idx], og.at[idx], s_o, r_o.at[idx], dev)

    def z_out(n):
        i = slab(s, t, z)
        rows = pl.ds(pl.multiple_of(t * OR, OR), OR)
        send(oproj_hbm.at[rows], og.at[i], s_oz, r_o.at[i], {"tp": n})

    def z_to(d):
        @pl.when(z + d < N)
        def _():
            z_out(jnp.minimum(z + d, N - 1))

        @pl.when(z - d >= 0)
        def _():
            z_out(jnp.maximum(z - d, 0))

    mid = (z == h - 1) | (z == h)
    lens = [lengths[k] for k in range(S)]
    offs = []
    total = jnp.int32(0)
    for k in range(S):
        offs.append(total)
        total = total + lens[k]
    own_off = jnp.int32(0)
    own_len = jnp.int32(0)
    for k in range(S):
        own_off = own_off + jnp.where(s == k, offs[k], 0)
        own_len = own_len + jnp.where(s == k, lens[k], 0)

    RB = 16 if RR % 16 == 0 else 8
    KC = chunk_of(D, 1024)

    def norm_rows(slot, first, count):
        def body(i, carry):
            rows = pl.ds(pl.multiple_of(first + i * RB, RB), RB)
            v = xbuf[slot, rows, :].astype(F32)
            inv = lax.rsqrt(jnp.sum(v * v, axis=1, keepdims=True) * (1.0 / D) + EPSILON)
            nbuf[slot, rows, :] = (v * inv * igain[...]).astype(BF16)
            return carry

        lax.fori_loop(0, count // RB, body, 0)

    def head_norm(v, gain):
        inv = lax.rsqrt(jnp.mean(v * v, axis=1, keepdims=True) + EPSILON)
        return v * inv * gain

    def project(slot, j):
        def body(i, acc):
            ks = pl.ds(pl.multiple_of(i * KC, KC), KC)
            return acc + jnp.dot(nbuf[slot, :, ks], w[j, ks, :], preferred_element_type=F32)

        v = lax.fori_loop(0, D // KC, body, jnp.zeros((R, 3 * HW), F32))
        co, si = cos_t[slot], sin_t[slot]

        def rope(u):
            return u * co + pltpu.roll(u, HW // 2, 1) * si

        q = (rope(head_norm(v[:, :HW], qgain[...])) * QUERY_SCALE).astype(BF16)
        k = rope(head_norm(v[:, HW : 2 * HW], kgain[...])).astype(BF16)
        return q, jnp.concatenate([k, v[:, 2 * HW :].astype(BF16)], axis=1)

    def share(n):
        for k in xs:
            send(kv_all.at[s, n], kv_all.at[s, n], s_kvx, r_kvx.at[s], {"seq": k})

    def own_head(slot):
        q, kv = project(slot, 0)
        n = p * h + slot
        q_all[n] = q
        kv_all[s, n] = kv
        share(n)

    def other_head(slot, late=1):
        q, kv = project(slot, 1)
        n = p * h + slot
        q_snd[slot] = q
        kv_snd[slot] = kv
        send(kv_snd.at[slot], kv_all.at[s, n], s_kv, r_kv.at[late], {"tp": zp})
        send(q_snd.at[slot], q_all.at[n], s_q, r_q, {"tp": zp})

    def tables():
        loc[3].wait()
        loc[4].wait()
        for k in range(D // 128):
            igain[0:1, k * 128 : (k + 1) * 128] = igs[k : k + 1, :]
            pgain[0:1, k * 128 : (k + 1) * 128] = pgs[k : k + 1, :]
        lane = lax.broadcasted_iota(jnp.int32, (R, HW), 1)
        for k in range(h):
            row = lax.broadcasted_iota(jnp.int32, (R, HW), 0)
            angle = (PREFIX + own_off + (p * h + k) * R + row).astype(F32) * freq[...]
            cos_t[k] = jnp.cos(angle)
            sine = jnp.sin(angle)
            sin_t[k] = jnp.where(lane < HW // 2, -sine, sine)
        loc[0].wait()
        norm_rows(b, 0, R)
        loc[1].wait()
        loc[2].wait()
        own_head(b)
        for k in range(T):
            loc[6 + k].wait()
    def plane(n):
        i = slab(s, t, n)
        arrived(og.at[i], r_o.at[i])
        for k in xs:
            o_copy(i, {"seq": k})
        for k in ys:
            o_copy(i, {"tmpl": k})
        o_copy(i, {"tmpl": tc})

    def each(d, fn):
        @pl.when(z + d < N)
        def _():
            fn(z + d)

        @pl.when(z - d >= 0)
        def _():
            fn(z - d)

    def from_x(n, diag=True):
        for ks in xs:
            i = slab(ks, t, n)
            arrived(og.at[i], r_o.at[i])
            if diag:
                for k in ys:
                    o_copy(i, {"tmpl": k})
            o_copy(i, {"tmpl": tc})

    def from_y(n, diag=False):
        for kt in ys:
            i = slab(s, kt, n)
            arrived(og.at[i], r_o.at[i])
            if diag:
                for k in xs:
                    o_copy(i, {"seq": k})
            o_copy(i, {"tmpl": tc})

    def from_diag(n):
        for kt in ys:
            for ks in xs:
                i = slab(ks, kt, n)
                arrived(og.at[i], r_o.at[i])
                o_copy(i, {"tmpl": tc})

    def from_c(n, own=False):
        for kt in cross:
            for ks in xs if own else [s] + xs:
                i = slab(ks, kt, n)
                arrived(og.at[i], r_o.at[i])

    def w_send(e_t, e_s, c, dev):
        pc = piece(e_t, e_s, c)
        send(w.at[1, pc], w.at[1, pc], s_w, r_w.at[e_t, e_s, c], dev)

    def w_own(c):
        arrived(w.at[1, piece(t, sb, c)], r_own.at[c])
        for k in x2:
            w_send(t, sb, c, {"seq": sg + k})
        for k in ys:
            w_send(t, sb, c, {"tmpl": k})
        w_send(t, sb, c, {"tmpl": tc})

    def w_got(e_t, e_s, c):
        arrived(w.at[1, piece(e_t, e_s, c)], r_w.at[e_t, e_s, c])

    def w_one(c):
        for k2 in x2:
            w_got(t, k2, c)
            if c % 2 == 0:
                for k in ys:
                    w_send(t, k2, c, {"tmpl": k})
            w_send(t, k2, c, {"tmpl": tc})
        for kt in ys:
            w_got(kt, sb, c)
            if c % 2 == 1:
                for k in x2:
                    w_send(kt, sb, c, {"seq": sg + k})
            w_send(kt, sb, c, {"tmpl": tc})

    def w_two(c):
        for kt in ys:
            for k2 in x2:
                w_got(kt, k2, c)
                w_send(kt, k2, c, {"tmpl": tc})

    def take_rows(slot):
        for c in range(RC):
            rows = pl.ds(c * RR, RR)
            arrived(xbuf.at[slot, rows], r_x.at[slot, c])
            norm_rows(slot, c * RR, RR)

    def w_cross():
        for c in range(NC):
            for kt in cross:
                for ks in range(S2):
                    w_got(kt, ks, c)

    def send_cache():
        for k in xs:
            send(cache_hbm, cbuf.at[s], s_c, r_c.at[s], {"seq": k})

    def send_own():
        rows = pl.ds(pl.multiple_of(t * OR, OR), OR)
        i = slab(s, t, z)
        for k in xs:
            send(oproj_hbm.at[rows], og.at[i], s_o, r_o.at[i], {"seq": k})

    def other_rows():
        for k in range(1, h):
            take_rows((b + k) % h)
            other_head((b + k) % h)

    def own_rows():
        for k in range(1, h):
            own_head((b + k) % h)

    def wait_early():
        n = op * h + b
        arrived(kv_all.at[s, n], r_kv.at[0])
        share(n)

    def wait_kv():
        arrived(kv_all.at[s, pl.ds(op * h, h - 1)], r_kv.at[1])
        for k in range(1, h):
            share(op * h + (b + k) % h)
        arrived(q_all.at[pl.ds(op * h, h)], r_q)

    def wait_kvx():
        loc[5].wait()
        for k in xs:
            arrived(cbuf.at[k], r_c.at[k])
            arrived(kv_all.at[k], r_kvx.at[k])

    def attend(d, carry):
        n = lax.rem(z + d, N)
        q = q_all[n]
        slot_c = n * R + lax.broadcasted_iota(jnp.int32, (R, 1), 0)
        pos = PREFIX + own_off + slot_c
        scores, values = [], []
        for k in range(S):
            cb = cbuf[k]
            sc = lax.dot_general(
                q, cb[:, :HW], (((1,), (1,)), ((), ())), preferred_element_type=F32
            )
            kp = PREFIX - WIN + k * C + lax.broadcasted_iota(jnp.int32, (1, C), 1)
            scores.append(jnp.where(kp > pos - WIN, sc, MASKED))
            values.append(cb[:, HW:])
            kv = flat(kv_all[k])
            sc = lax.dot_general(
                q, kv[:, :HW], (((1,), (1,)), ((), ())), preferred_element_type=F32
            )
            j = lax.broadcasted_iota(jnp.int32, (1, N * R), 1)
            kp = PREFIX + offs[k] + j
            kp = jnp.where(j < lens[k], kp, PREFIX + WIN + S * N * R)
            ok = kp <= pos
            if S * N * R > WIN:
                ok = ok & (kp > pos - WIN)
            scores.append(jnp.where(ok, sc, MASKED))
            values.append(kv[:, HW:])
        top = functools.reduce(
            jnp.maximum, [jnp.max(v, axis=1, keepdims=True) for v in scores]
        )
        row_sum = jnp.zeros((R, 1), F32)
        acc = jnp.zeros((R, HW), F32)
        for sc, vv in zip(scores, values):
            wt = jnp.exp(sc - top)
            row_sum = row_sum + jnp.sum(wt, axis=1, keepdims=True)
            acc = acc + jnp.dot(wt.astype(BF16), vv, preferred_element_type=F32)
        live = slot_c < own_len
        res = acc / jnp.where(live, row_sum, 1.0)
        hsnd[n] = jnp.where(live, res, 0.0).astype(BF16)

        @pl.when(d < N)
        def _():
            send(hsnd.at[n], ho.at[z], s_h, r_h, {"tp": n})

        return carry

    def attention():
        lax.fori_loop(1, N + 1, attend, 0)
        ho[z] = hsnd[z]

    def dist(k):
        return [d for d in range(1, N) if d == k or (k == 3 and d > 3)]

    ops = {
        "SW": send_w, "OWN": tables, "SC": send_cache, "SO": send_own, "WC": w_cross,
        "OB": lambda: other_head(b, 0), "KE": wait_early, "RN": other_rows, "ON": own_rows, "KV": wait_kv,
        "KX": wait_kvx, "AT": attention, "XZ": lambda: from_x(z), "DZ": lambda: from_diag(z),
    }

    def step(tok):
        if tok in ops:
            return ops[tok]()
        kind, k = tok[0], int(tok[1])
        if kind in "WAB":
            if k < NC:
                (w_own if kind == "W" else w_one if kind == "A" else w_two)(k)
        elif kind == "R":
            if k < RC:
                send_rows(k)
        else:
            via_x = k in VIA_X
            for d in dist(k):
                if kind == "Z":
                    z_to(d)
                elif kind == "P":
                    each(d, plane)
                elif kind == "X":
                    each(d, lambda n: from_x(n, not via_x))
                elif kind == "Y":
                    each(d, lambda n: from_y(n, via_x))
                elif kind == "D":
                    each(d, from_diag)

    kinds = [(0, False), (0, True), (1, False), (1, True)]
    plans = [PLANS[k] for k in kinds]
    first = 0
    while all(len(q) > first and q[first] == plans[0][first] for q in plans):
        step(plans[0][first])
        first += 1
    last = 0
    while all(len(q) > first + last and q[-1 - last] == plans[0][-1 - last] for q in plans):
        last += 1
    for (kp, km), q in zip(kinds, plans):
        if len(q) > first + last:
            @pl.when((par == kp) & (mid == km))
            def _():
                for tok in q[first : len(q) - last]:
                    step(tok)
    for tok in plans[0][len(plans[0]) - last :]:
        step(tok)
    from_c(z, True)
    for d in range(1, N):
        each(d, from_c)
    arrived(ho.at[pl.ds(0, N - 1)], r_h)

    CC = chunk_of(DC, 1024)

    def partial(first, k, cs):
        acc = None
        for g in range(0, h, 2):
            n = first + g
            wt = jnp.concatenate(
                [og[slab(k, kt, n + j), :, cs] for j in range(2) for kt in range(T)], axis=0
            )
            hv = jnp.concatenate([ho[n + j] for j in range(2)], axis=1)
            v = jnp.dot(hv, wt, preferred_element_type=F32)
            acc = v if acc is None else acc + v
        return acc

    for k in range(S):
        def cols(i, carry):
            cs = pl.ds(pl.multiple_of(i * CC, CC), CC)
            proj[:, pl.ds(pl.multiple_of(k * DC + i * CC, 128), CC)] = (
                partial(p * h, k, cs) + partial(op * h, k, cs)
            )
            return carry

        lax.fori_loop(0, DC // CC, cols, 0)

    RF = 16 if R % 16 == 0 else 8

    def finish(i, carry):
        rows = pl.ds(pl.multiple_of(i * RF, RF), RF)
        v = proj[rows, :]
        inv = lax.rsqrt(jnp.sum(v * v, axis=1, keepdims=True) * (1.0 / D) + EPSILON)
        obuf[rows, :] = (xbuf[b, rows, :].astype(F32) + v * inv * pgain[...]).astype(BF16)
        pltpu.make_async_copy(obuf.at[rows], out_ref.at[rows], osem).start()
        return carry

    lax.fori_loop(0, R // RF, finish, 0)

    pltpu.make_async_copy(obuf, out_ref, osem).wait()
    left(w.at[1], s_w)
    left(xbuf.at[pl.ds(0, h - 1)], s_x)
    left(cbuf.at[pl.ds(0, S - 1)], s_c)
    left(kv_all.at[pl.ds(0, S - 1)], s_kvx)
    left(kv_snd, s_kv)
    left(q_snd, s_q)
    left(hsnd.at[pl.ds(0, N - 1)], s_h)
    X, Y = S - 1, T // 2 - 1
    count = (N - 1) * (X + Y + 1 + X * (Y + 1) + Y * S) + (Y + 1) * X * 2
    while count > 0:
        part = min(count, S * T * N)
        left(og.at[pl.ds(0, part)], s_o)
        count -= part
    left(og.at[pl.ds(0, N - 1)], s_oz)


def shards(
    T, S, N,
    tokens, lengths, input_gain, query_proj, key_value, query_gain, key_gain,
    window_cache, output_proj, post_gain,
):
    R, D = tokens.shape
    HW = query_proj.shape[1]
    C = window_cache.shape[0]
    h = N // 2
    S2 = max(d for d in range(1, S + 1) if S % d == 0 and D % (16 * T * d) == 0)
    NC = max(d for d in (1, 2, 3, 6) if D // (T * S2) % (16 * d) == 0)
    RC = 3 if R % 48 == 0 else 1
    inv = np.power(ROPE_BASE, -2.0 * np.arange(HW // 2) / HW)
    freq = np.concatenate([inv, inv])[None, :].astype(np.float32)
    OR, DC = output_proj.shape[0] // T, output_proj.shape[1]
    vm = pl.BlockSpec(memory_space=pltpu.VMEM)
    hb = pl.BlockSpec(memory_space=pltpu.HBM)
    dma = pltpu.SemaphoreType.DMA
    return pl.pallas_call(
        functools.partial(kernel, T, S, N, S2, NC, RC),
        out_shape=jax.ShapeDtypeStruct((R, D), BF16),
        in_specs=[pl.BlockSpec(memory_space=pltpu.SMEM), hb, hb, hb, hb, hb]
        + [hb, hb, vm, vm, vm],
        out_specs=hb,
        scratch_shapes=[
            pltpu.VMEM((D // 128, 128), F32),
            pltpu.VMEM((D // 128, 128), F32),
            pltpu.VMEM((1, D), F32),
            pltpu.VMEM((1, D), F32),
            pltpu.VMEM((h, R, HW), F32),
            pltpu.VMEM((h, R, HW), F32),
            pltpu.VMEM((h, R, D), BF16),
            pltpu.VMEM((h, R, D), BF16),
            pltpu.VMEM((2, D, 3 * HW), BF16),
            pltpu.VMEM((S, C, 2 * HW), BF16),
            pltpu.VMEM((S * T * N, OR, DC), BF16),
            pltpu.VMEM((N, R, HW), BF16),
            pltpu.VMEM((S, N, R, 2 * HW), BF16),
            pltpu.VMEM((h, R, HW), BF16),
            pltpu.VMEM((h, R, 2 * HW), BF16),
            pltpu.VMEM((N, R, HW), BF16),
            pltpu.VMEM((N, R, HW), BF16),
            pltpu.VMEM((R, D), F32),
            pltpu.VMEM((R, D), BF16),
            dma((6 + T,)), dma, dma, dma, dma, dma, dma, dma, dma, dma, dma,
            dma((h, RC)), dma((S,)), dma((NC,)), dma((T, S2, NC)), dma((S * T * N,)),
            dma, dma((2,)), dma((S,)), dma,
        ],
        compiler_params=pltpu.CompilerParams(
            collective_id=0, has_side_effects=True, vmem_limit_bytes=67043328 - R * D * 2
        ),
    )(
        lengths, tokens, query_proj, key_value, window_cache, output_proj,
        input_gain.reshape(D // 128, 128), post_gain.reshape(D // 128, 128),
        query_gain[None, :], key_gain[None, :], jnp.asarray(freq),
    )


def solution(mesh):
    T, S, N = mesh.shape["tmpl"], mesh.shape["seq"], mesh.shape["tp"]
    return jax.shard_map(
        functools.partial(shards, T, S, N),
        mesh=mesh,
        in_specs=(
            P(("tmpl", "seq", "tp"), None),
            P("tmpl"),
            P(),
            P(None, "tp"),
            P(None, "tp"),
            P(),
            P(),
            P(("tmpl", "seq"), "tp"),
            P("tp", "seq"),
            P(),
        ),
        out_specs=P(("tmpl", "seq", "tp"), None),
        check_vma=False,
    )
```

```python
import functools

import jax
import jax.numpy as jnp
import numpy as np
from jax import lax
from jax.experimental import pallas as pl
from jax.experimental.pallas import tpu as pltpu
from jax.sharding import PartitionSpec as P

WIN = 1024
PREFIX = 32768
EPSILON = 1e-06
ROPE_BASE = 10000.0
QUERY_SCALE = 168.0 ** (-0.5)
MASKED = -1e30
F32 = jnp.float32
BF16 = jnp.bfloat16
MESH = pl.DeviceIdType.MESH


VIA_X = ()
PLANS = {
    (0, False): (
        "SW", "Z1", "R0", "R1", "Z2", "R2", "Z3", "SO", "SC", "W0", "OWN", "W1",
        "A0", "W2", "A1", "B0", "W3", "A2", "B1", "W4", "A3", "B2", "XZ", "W5",
        "A4", "B3", "A5", "B4", "P1", "B5", "P2", "WC", "OB", "RN", "X1", "ON",
        "KE", "X2", "P3", "Y1", "KV", "X3", "KX", "AT", "D1", "DZ", "Y2", "D2",
        "Y3", "D3",
    ),
    (0, True): (
        "SW", "R0", "R1", "R2", "Z1", "Z2", "Z3", "SO", "OWN", "W0", "W1", "A0",
        "W2", "A1", "B0", "W3", "A2", "B1", "W4", "A3", "B2", "XZ", "W5", "A4",
        "B3", "A5", "B4", "P1", "B5", "SC", "WC", "OB", "X1", "RN", "P2", "P3",
        "ON", "KE", "Y1", "KV", "X2", "X3", "KX", "AT", "D1", "DZ", "Y2", "D2",
        "Y3", "D3",
    ),
    (1, False): (
        "R0", "SW", "Z1", "R1", "R2", "Z2", "SO", "SC", "W0", "W1", "A0", "W2",
        "A1", "B0", "OWN", "W3", "A2", "B1", "W4", "A3", "B2", "XZ", "W5", "A4",
        "B3", "A5", "B4", "P1", "B5", "P2", "WC", "OB", "Z3", "KE", "X1", "X2",
        "RN", "ON", "Y1", "KV", "P3", "KX", "X3", "AT", "D1", "DZ", "Y2", "D2",
        "Y3", "D3",
    ),
    (1, True): (
        "SW", "SO", "OWN", "W0", "W1", "A0", "W2", "A1", "B0", "W3", "A2", "B1",
        "W4", "A3", "B2", "XZ", "W5", "A4", "B3", "Z1", "R0", "R1", "R2", "Z2",
        "Z3", "A5", "B4", "P1", "B5", "SC", "WC", "OB", "X1", "RN", "P2", "P3",
        "ON", "KE", "Y1", "KV", "X2", "X3", "KX", "AT", "D1", "DZ", "Y2", "D2",
        "Y3", "D3",
    ),
}


def chunk_of(width, limit):
    best = 128
    for c in range(128, limit + 1, 128):
        if width % c == 0:
            best = c
    return best


def flat(v):
    shape = (v.shape[0] * v.shape[1], v.shape[2])
    if v.shape[1] % 16 == 0:
        return v.reshape(shape)
    return v.astype(F32).reshape(shape).astype(v.dtype)


def kernel(
    T, S, N, S2, NC, RC,
    lengths, tokens, wq_hbm, wkv_hbm, cache_hbm, oproj_hbm,
    ig_hbm, pg_hbm, qgain, kgain, freq,
    out_ref,
    igs, pgs, igain, pgain, cos_t, sin_t, xbuf, nbuf, w, cbuf, og, q_all, kv_all, q_snd, kv_snd, hsnd, ho, proj, obuf,
    lsem, osem, s_w, s_x, s_c, s_o, s_oz, s_kvx, s_kv, s_q, s_h,
    r_x, r_c, r_own, r_w, r_wc, r_o, r_oc, r_q, r_kv, r_kvx, r_h,
):
    t, s, z = lax.axis_index("tmpl"), lax.axis_index("seq"), lax.axis_index("tp")
    h = N // 2
    p, b = z // h, z % h
    op = 1 - p
    zp = (z + h) % N
    R, D = tokens.shape
    HW = wq_hbm.shape[1]
    C = cache_hbm.shape[0]
    DE = D // (T * S2)
    DN = DE // NC
    RR = R // RC
    OR = oproj_hbm.shape[0] // T
    DC = oproj_hbm.shape[1]
    tc = t + 1 - 2 * (t % 2)
    par = t % 2
    ys = [(t + 2 * k) % T for k in range(1, T // 2)]
    xs = [(s + k) % S for k in range(1, S)]
    sg, sb = (s // S2) * S2, s % S2
    x2 = [(sb + k) % S2 for k in range(1, S2)]
    zs = [(z + k) % N for k in range(1, N)]

    def copy(src, dst, ssem, rsem, dev):
        return pltpu.make_async_remote_copy(
            src_ref=src, dst_ref=dst, send_sem=ssem, recv_sem=rsem,
            device_id=dev, device_id_type=MESH,
        )

    def send(src, dst, ssem, rsem, dev):
        copy(src, dst, ssem, rsem, dev).start()

    def arrived(dst, rsem):
        copy(dst, dst, s_q, rsem, {"tp": zp}).wait_recv()

    def left(src, ssem):
        copy(src, src, ssem, r_q, {"tp": zp}).wait_send()

    loc = [
        pltpu.make_async_copy(tokens, xbuf.at[b], lsem.at[0]),
        pltpu.make_async_copy(wq_hbm, w.at[0, :, pl.ds(0, HW)], lsem.at[1]),
        pltpu.make_async_copy(wkv_hbm, w.at[0, :, pl.ds(HW, 2 * HW)], lsem.at[2]),
        pltpu.make_async_copy(ig_hbm, igs, lsem.at[3]),
        pltpu.make_async_copy(pg_hbm, pgs, lsem.at[4]),
        pltpu.make_async_copy(cache_hbm, cbuf.at[s], lsem.at[5]),
    ]

    def slab(ks, kt, n):
        return (ks * T + kt) * N + n

    def slot_of(ks, kt, n):
        return (ks * (T // 2) + kt // 2) * N + n

    for k in range(T):
        loc.append(
            pltpu.make_async_copy(
                oproj_hbm.at[pl.ds(k * OR, OR)], og.at[slab(s, k, z)], lsem.at[6]
            )
        )
    for c in loc:
        c.start()

    barrier = pltpu.get_barrier_semaphore()
    peers = (
        [{"tp": k} for k in zs] + [{"seq": k} for k in xs]
        + [{"tmpl": k} for k in ys] + [{"tmpl": tc}]
    )
    for dev in peers:
        pl.semaphore_signal(barrier, inc=1, device_id=dev, device_id_type=MESH)
    pl.semaphore_wait(barrier, len(peers))

    def piece(e_t, e_s, c):
        return pl.ds(pl.multiple_of((e_t * S2 + e_s) * DE + c * DN, DN), DN)

    def send_w():
        for c in range(NC):
            pc = piece(t, sb, c)
            for src, at in ((wq_hbm, pl.ds(0, HW)), (wkv_hbm, pl.ds(HW, 2 * HW))):
                send(src.at[pc], w.at[1, pc, at], s_w, r_own.at[c], {"tp": zp})

    def send_rows(c):
        rows = pl.ds(c * RR, RR)
        for k in range(1, h):
            send(tokens.at[rows], xbuf.at[b, rows], s_x, r_x.at[b, c], {"tp": p * h + (b + k) % h})

    pt = jnp.where(z < h, jnp.where(z == h - 1, h, h - 1), jnp.where(z == h, h - 1, h))

    def o_copy(ks, kt, n, dev):
        i = slab(ks, kt, n)
        if "tmpl" in dev and dev["tmpl"] is tc:
            sem = r_oc.at[jnp.where((n == z) | (n == pt), 0, 1)]
        else:
            sem = r_o.at[slot_of(ks, kt, n)]
        send(og.at[i], og.at[i], s_o, sem, dev)

    def o_got(ks, kt, n):
        arrived(og.at[slab(ks, kt, n)], r_o.at[slot_of(ks, kt, n)])

    def z_out(n):
        rows = pl.ds(pl.multiple_of(t * OR, OR), OR)
        send(oproj_hbm.at[rows], og.at[slab(s, t, z)], s_oz, r_o.at[slot_of(s, t, z)], {"tp": n})

    def z_to(d):
        @pl.when(z + d < N)
        def _():
            z_out(jnp.minimum(z + d, N - 1))

        @pl.when(z - d >= 0)
        def _():
            z_out(jnp.maximum(z - d, 0))

    mid = (z == h - 1) | (z == h)
    lens = [lengths[k] for k in range(S)]
    offs = []
    total = jnp.int32(0)
    for k in range(S):
        offs.append(total)
        total = total + lens[k]
    own_off = jnp.int32(0)
    own_len = jnp.int32(0)
    for k in range(S):
        own_off = own_off + jnp.where(s == k, offs[k], 0)
        own_len = own_len + jnp.where(s == k, lens[k], 0)

    RB = 16 if RR % 16 == 0 else 8
    KC = chunk_of(D, 1024)

    def norm_rows(slot, first, count):
        def body(i, carry):
            rows = pl.ds(pl.multiple_of(first + i * RB, RB), RB)
            v = xbuf[slot, rows, :].astype(F32)
            inv = lax.rsqrt(jnp.sum(v * v, axis=1, keepdims=True) * (1.0 / D) + EPSILON)
            nbuf[slot, rows, :] = (v * inv * igain[...]).astype(BF16)
            return carry

        lax.fori_loop(0, count // RB, body, 0)

    def head_norm(v, gain):
        inv = lax.rsqrt(jnp.mean(v * v, axis=1, keepdims=True) + EPSILON)
        return v * inv * gain

    def project(slot, j):
        def body(i, acc):
            ks = pl.ds(pl.multiple_of(i * KC, KC), KC)
            return acc + jnp.dot(nbuf[slot, :, ks], w[j, ks, :], preferred_element_type=F32)

        v = lax.fori_loop(0, D // KC, body, jnp.zeros((R, 3 * HW), F32))
        co, si = cos_t[slot], sin_t[slot]

        def rope(u):
            return u * co + pltpu.roll(u, HW // 2, 1) * si

        q = (rope(head_norm(v[:, :HW], qgain[...])) * QUERY_SCALE).astype(BF16)
        k = rope(head_norm(v[:, HW : 2 * HW], kgain[...])).astype(BF16)
        return q, jnp.concatenate([k, v[:, 2 * HW :].astype(BF16)], axis=1)

    def share(n):
        for k in xs:
            send(kv_all.at[s, n], kv_all.at[s, n], s_kvx, r_kvx.at[s], {"seq": k})

    def own_head(slot):
        q, kv = project(slot, 0)
        n = p * h + slot
        q_all[n] = q
        kv_all[s, n] = kv
        share(n)

    def other_head(slot, late=1):
        q, kv = project(slot, 1)
        n = p * h + slot
        q_snd[slot] = q
        kv_snd[slot] = kv
        send(kv_snd.at[slot], kv_all.at[s, n], s_kv, r_kv.at[late], {"tp": zp})
        send(q_snd.at[slot], q_all.at[n], s_q, r_q, {"tp": zp})

    def tables():
        loc[3].wait()
        loc[4].wait()
        for k in range(D // 128):
            igain[0:1, k * 128 : (k + 1) * 128] = igs[k : k + 1, :]
            pgain[0:1, k * 128 : (k + 1) * 128] = pgs[k : k + 1, :]
        lane = lax.broadcasted_iota(jnp.int32, (R, HW), 1)
        for k in range(h):
            row = lax.broadcasted_iota(jnp.int32, (R, HW), 0)
            angle = (PREFIX + own_off + (p * h + k) * R + row).astype(F32) * freq[...]
            cos_t[k] = jnp.cos(angle)
            sine = jnp.sin(angle)
            sin_t[k] = jnp.where(lane < HW // 2, -sine, sine)
        loc[0].wait()
        norm_rows(b, 0, R)
        loc[1].wait()
        loc[2].wait()
        own_head(b)
        pltpu.make_async_copy(og.at[pl.ds(0, T)], og.at[pl.ds(0, T)], lsem.at[6]).wait()
    def plane(n):
        o_got(s, t, n)
        for k in xs:
            o_copy(s, t, n, {"seq": k})
        for k in ys:
            o_copy(s, t, n, {"tmpl": k})
        o_copy(s, t, n, {"tmpl": tc})

    def each(d, fn):
        @pl.when(z + d < N)
        def _():
            fn(z + d)

        @pl.when(z - d >= 0)
        def _():
            fn(z - d)

    def from_x(n, diag=True):
        for ks in xs:
            o_got(ks, t, n)
            if diag:
                for k in ys:
                    o_copy(ks, t, n, {"tmpl": k})
            o_copy(ks, t, n, {"tmpl": tc})

    def from_y(n, diag=False):
        for kt in ys:
            o_got(s, kt, n)
            if diag:
                for k in xs:
                    o_copy(s, kt, n, {"seq": k})
            o_copy(s, kt, n, {"tmpl": tc})

    def from_diag(n):
        for kt in ys:
            for ks in xs:
                o_got(ks, kt, n)
                o_copy(ks, kt, n, {"tmpl": tc})

    def w_send(e_t, e_s, c, dev):
        pc = piece(e_t, e_s, c)
        sem = r_wc if "tmpl" in dev and dev["tmpl"] is tc else r_w.at[e_t // 2, e_s, c]
        send(w.at[1, pc], w.at[1, pc], s_w, sem, dev)

    def w_own(c):
        arrived(w.at[1, piece(t, sb, c)], r_own.at[c])
        for k in x2:
            w_send(t, sb, c, {"seq": sg + k})
        for k in ys:
            w_send(t, sb, c, {"tmpl": k})
        w_send(t, sb, c, {"tmpl": tc})

    def w_got(e_t, e_s, c):
        arrived(w.at[1, piece(e_t, e_s, c)], r_w.at[e_t // 2, e_s, c])

    def w_one(c):
        for k2 in x2:
            w_got(t, k2, c)
            if c % 2 == 0:
                for k in ys:
                    w_send(t, k2, c, {"tmpl": k})
            w_send(t, k2, c, {"tmpl": tc})
        for kt in ys:
            w_got(kt, sb, c)
            if c % 2 == 1:
                for k in x2:
                    w_send(kt, sb, c, {"seq": sg + k})
            w_send(kt, sb, c, {"tmpl": tc})

    def w_two(c):
        for kt in ys:
            for k2 in x2:
                w_got(kt, k2, c)
                w_send(kt, k2, c, {"tmpl": tc})

    def take_rows(slot):
        for c in range(RC):
            rows = pl.ds(c * RR, RR)
            arrived(xbuf.at[slot, rows], r_x.at[slot, c])
            norm_rows(slot, c * RR, RR)

    def w_cross():
        arrived(w.at[1, pl.ds(0, D // 2)], r_wc)

    def send_cache():
        for k in xs:
            send(cache_hbm, cbuf.at[s], s_c, r_c.at[s], {"seq": k})

    def send_own():
        rows = pl.ds(pl.multiple_of(t * OR, OR), OR)
        i = slab(s, t, z)
        for k in xs:
            send(oproj_hbm.at[rows], og.at[i], s_o, r_o.at[slot_of(s, t, z)], {"seq": k})

    def other_rows():
        for k in range(1, h):
            take_rows((b + k) % h)
            other_head((b + k) % h)

    def own_rows():
        for k in range(1, h):
            own_head((b + k) % h)

    def wait_early():
        n = op * h + b
        arrived(kv_all.at[s, n], r_kv.at[0])
        share(n)

    def wait_kv():
        arrived(kv_all.at[s, pl.ds(op * h, h - 1)], r_kv.at[1])
        for k in range(1, h):
            share(op * h + (b + k) % h)
        arrived(q_all.at[pl.ds(op * h, h)], r_q)

    def wait_kvx():
        loc[5].wait()
        for k in xs:
            arrived(cbuf.at[k], r_c.at[k])
            arrived(kv_all.at[k], r_kvx.at[k])

    def attend(d, carry):
        m = lax.rem(z // 2 + d, h)
        q = flat(q_all[pl.ds(2 * m, 2)])
        slot_c = 2 * m * R + lax.broadcasted_iota(jnp.int32, (2 * R, 1), 0)
        pos = PREFIX + own_off + slot_c
        scores, values = [], []
        for k in range(S):
            cb = cbuf[k]
            sc = lax.dot_general(
                q, cb[:, :HW], (((1,), (1,)), ((), ())), preferred_element_type=F32
            )
            kp = PREFIX - WIN + k * C + lax.broadcasted_iota(jnp.int32, (1, C), 1)
            scores.append(jnp.where(kp > pos - WIN, sc, MASKED))
            values.append(cb[:, HW:])
            kv = flat(kv_all[k])
            sc = lax.dot_general(
                q, kv[:, :HW], (((1,), (1,)), ((), ())), preferred_element_type=F32
            )
            j = lax.broadcasted_iota(jnp.int32, (1, N * R), 1)
            kp = PREFIX + offs[k] + j
            kp = jnp.where(j < lens[k], kp, PREFIX + WIN + S * N * R)
            ok = kp <= pos
            if S * N * R > WIN:
                ok = ok & (kp > pos - WIN)
            scores.append(jnp.where(ok, sc, MASKED))
            values.append(kv[:, HW:])
        top = functools.reduce(
            jnp.maximum, [jnp.max(v, axis=1, keepdims=True) for v in scores]
        )
        row_sum = jnp.zeros((2 * R, 1), F32)
        acc = jnp.zeros((2 * R, HW), F32)
        for sc, vv in zip(scores, values):
            wt = jnp.exp(sc - top)
            row_sum = row_sum + jnp.sum(wt, axis=1, keepdims=True)
            acc = acc + jnp.dot(wt.astype(BF16), vv, preferred_element_type=F32)
        live = slot_c < own_len
        res = acc / jnp.where(live, row_sum, 1.0)
        res = jnp.where(live, res, 0.0).astype(BF16)
        for j in range(2):
            hsnd[2 * m + j] = res[j * R : (j + 1) * R]
        for j in range(2):
            n = 2 * m + j

            @pl.when(n != z)
            def _():
                send(hsnd.at[n], ho.at[z], s_h, r_h.at[z], {"tp": n})

        return carry

    def attention():
        lax.fori_loop(1, h + 1, attend, 0)
        ho[z] = hsnd[z]

    def dist(k):
        return [d for d in range(1, N) if d == k or (k == 3 and d > 3)]

    ops = {
        "SW": send_w, "OWN": tables, "SC": send_cache, "SO": send_own, "WC": w_cross,
        "OB": lambda: other_head(b, 0), "KE": wait_early, "RN": other_rows, "ON": own_rows, "KV": wait_kv,
        "KX": wait_kvx, "AT": attention, "XZ": lambda: from_x(z), "DZ": lambda: from_diag(z),
    }

    def step(tok):
        if tok in ops:
            return ops[tok]()
        kind, k = tok[0], int(tok[1])
        if kind in "WAB":
            if k < NC:
                (w_own if kind == "W" else w_one if kind == "A" else w_two)(k)
        elif kind == "R":
            if k < RC:
                send_rows(k)
        else:
            via_x = k in VIA_X
            for d in dist(k):
                if kind == "Z":
                    z_to(d)
                elif kind == "P":
                    each(d, plane)
                elif kind == "X":
                    each(d, lambda n: from_x(n, not via_x))
                elif kind == "Y":
                    each(d, lambda n: from_y(n, via_x))
                elif kind == "D":
                    each(d, from_diag)

    kinds = [(0, False), (0, True), (1, False), (1, True)]
    plans = [PLANS[k] for k in kinds]
    first = 0
    while all(len(q) > first and q[first] == plans[0][first] for q in plans):
        step(plans[0][first])
        first += 1
    last = 0
    while all(len(q) > first + last and q[-1 - last] == plans[0][-1 - last] for q in plans):
        last += 1
    for (kp, km), q in zip(kinds, plans):
        if len(q) > first + last:
            @pl.when((par == kp) & (mid == km))
            def _():
                for tok in q[first : len(q) - last]:
                    step(tok)
    for tok in plans[0][len(plans[0]) - last :]:
        step(tok)
    CC = chunk_of(DC, 1024)
    lo, hi = jnp.minimum(z, pt), jnp.maximum(z, pt)
    rest = []
    for j in range(N - 2):
        n = j + jnp.where(j >= lo, 1, 0)
        rest.append(n + jnp.where(n >= hi, 1, 0))

    def project_out(pair, more):
        hv = jnp.concatenate([ho[n] for n in pair], axis=1)
        for k in range(S):
            def cols(i, carry):
                cs = pl.ds(pl.multiple_of(i * CC, CC), CC)
                at = pl.ds(pl.multiple_of(k * DC + i * CC, 128), CC)
                wt = jnp.concatenate(
                    [og[slab(k, kt, n), :, cs] for n in pair for kt in range(T)], axis=0
                )
                v = jnp.dot(hv, wt, preferred_element_type=F32)
                proj[:, at] = proj[:, at] + v if more else v
                return carry

            lax.fori_loop(0, DC // CC, cols, 0)

    X, Y = S - 1, T // 2 - 1
    near = (X + S) * (T // 2)
    arrived(og.at[pl.ds(0, near)], r_oc.at[0])
    arrived(ho.at[pt], r_h.at[pt])
    project_out([z, pt], False)
    arrived(og.at[pl.ds(0, (N - 2) * S * (T // 2))], r_oc.at[1])
    for n in rest:
        arrived(ho.at[n], r_h.at[n])
    for j in range(0, N - 2, 2):
        project_out(rest[j : j + 2], True)

    RF = 16 if R % 16 == 0 else 8

    def finish(i, carry):
        rows = pl.ds(pl.multiple_of(i * RF, RF), RF)
        v = proj[rows, :]
        inv = lax.rsqrt(jnp.sum(v * v, axis=1, keepdims=True) * (1.0 / D) + EPSILON)
        obuf[rows, :] = (xbuf[b, rows, :].astype(F32) + v * inv * pgain[...]).astype(BF16)
        pltpu.make_async_copy(obuf.at[rows], out_ref.at[rows], osem).start()
        return carry

    lax.fori_loop(0, R // RF, finish, 0)

    pltpu.make_async_copy(obuf, out_ref, osem).wait()
    left(w.at[1], s_w)
    left(xbuf.at[pl.ds(0, h - 1)], s_x)
    left(cbuf.at[pl.ds(0, S - 1)], s_c)
    left(kv_all.at[pl.ds(0, S - 1)], s_kvx)
    left(kv_snd, s_kv)
    left(q_snd, s_q)
    left(hsnd.at[pl.ds(0, N - 1)], s_h)
    count = (N - 1) * (X + Y + 1 + X * (Y + 1) + Y * S) + (Y + 1) * X * 2
    while count > 0:
        part = min(count, S * T * N)
        left(og.at[pl.ds(0, part)], s_o)
        count -= part
    left(og.at[pl.ds(0, N - 1)], s_oz)


def shards(
    T, S, N,
    tokens, lengths, input_gain, query_proj, key_value, query_gain, key_gain,
    window_cache, output_proj, post_gain,
):
    R, D = tokens.shape
    HW = query_proj.shape[1]
    C = window_cache.shape[0]
    h = N // 2
    S2 = max(d for d in range(1, S + 1) if S % d == 0 and D % (16 * T * d) == 0)
    NC = max(d for d in (1, 2, 3, 6) if D // (T * S2) % (16 * d) == 0)
    RC = 3 if R % 48 == 0 else 1
    inv = np.power(ROPE_BASE, -2.0 * np.arange(HW // 2) / HW)
    freq = np.concatenate([inv, inv])[None, :].astype(np.float32)
    OR, DC = output_proj.shape[0] // T, output_proj.shape[1]
    vm = pl.BlockSpec(memory_space=pltpu.VMEM)
    hb = pl.BlockSpec(memory_space=pltpu.HBM)
    dma = pltpu.SemaphoreType.DMA
    return pl.pallas_call(
        functools.partial(kernel, T, S, N, S2, NC, RC),
        out_shape=jax.ShapeDtypeStruct((R, D), BF16),
        in_specs=[pl.BlockSpec(memory_space=pltpu.SMEM), hb, hb, hb, hb, hb]
        + [hb, hb, vm, vm, vm],
        out_specs=hb,
        scratch_shapes=[
            pltpu.VMEM((D // 128, 128), F32),
            pltpu.VMEM((D // 128, 128), F32),
            pltpu.VMEM((1, D), F32),
            pltpu.VMEM((1, D), F32),
            pltpu.VMEM((h, R, HW), F32),
            pltpu.VMEM((h, R, HW), F32),
            pltpu.VMEM((h, R, D), BF16),
            pltpu.VMEM((h, R, D), BF16),
            pltpu.VMEM((2, D, 3 * HW), BF16),
            pltpu.VMEM((S, C, 2 * HW), BF16),
            pltpu.VMEM((S * T * N, OR, DC), BF16),
            pltpu.VMEM((N, R, HW), BF16),
            pltpu.VMEM((S, N, R, 2 * HW), BF16),
            pltpu.VMEM((h, R, HW), BF16),
            pltpu.VMEM((h, R, 2 * HW), BF16),
            pltpu.VMEM((N, R, HW), BF16),
            pltpu.VMEM((N, R, HW), BF16),
            pltpu.VMEM((R, D), F32),
            pltpu.VMEM((R, D), BF16),
            dma((7,)), dma, dma, dma, dma, dma, dma, dma, dma, dma, dma,
            dma((h, RC)), dma((S,)), dma((NC,)), dma((T // 2, S2, NC)), dma, dma((S * T // 2 * N,)), dma((2,)),
            dma, dma((2,)), dma((S,)), dma((N,)),
        ],
        compiler_params=pltpu.CompilerParams(
            collective_id=0, has_side_effects=True, vmem_limit_bytes=67043328 - R * D * 2
        ),
    )(
        lengths, tokens, query_proj, key_value, window_cache, output_proj,
        input_gain.reshape(D // 128, 128), post_gain.reshape(D // 128, 128),
        query_gain[None, :], key_gain[None, :], jnp.asarray(freq),
    )


def solution(mesh):
    T, S, N = mesh.shape["tmpl"], mesh.shape["seq"], mesh.shape["tp"]
    return jax.shard_map(
        functools.partial(shards, T, S, N),
        mesh=mesh,
        in_specs=(
            P(("tmpl", "seq", "tp"), None),
            P("tmpl"),
            P(),
            P(None, "tp"),
            P(None, "tp"),
            P(),
            P(),
            P(("tmpl", "seq"), "tp"),
            P("tp", "seq"),
            P(),
        ),
        out_specs=P(("tmpl", "seq", "tp"), None),
        check_vma=False,
    )
```

```python
import functools

import jax
import jax.numpy as jnp
import numpy as np
from jax import lax
from jax.experimental import pallas as pl
from jax.experimental.pallas import tpu as pltpu
from jax.sharding import PartitionSpec as P

WIN = 1024
PREFIX = 32768
EPSILON = 1e-06
ROPE_BASE = 10000.0
QUERY_SCALE = 168.0 ** (-0.5)
MASKED = -1e30
F32 = jnp.float32
BF16 = jnp.bfloat16
MESH = pl.DeviceIdType.MESH


VIA_X = {(0, False): (), (0, True): (), (1, False): (1,), (1, True): ()}
PLANS = {
    (0, False): (
        "SW", "Z1", "R0", "R1", "Z2", "R2", "Z3", "SO", "SC", "W0", "OWN", "W1",
        "A0", "W2", "A1", "B0", "W3", "A2", "B1", "W4", "A3", "B2", "XZ", "W5",
        "A4", "B3", "A5", "B4", "P1", "B5", "P2", "WC", "OB", "RN", "X1", "ON",
        "KE", "X2", "P3", "Y1", "KV", "X3", "KX", "AT", "D1", "DZ", "Y2", "D2",
        "Y3", "D3",
    ),
    (0, True): (
        "SW", "R0", "R1", "R2", "Z1", "Z2", "Z3", "SO", "OWN", "W0", "W1", "A0",
        "W2", "A1", "B0", "W3", "A2", "B1", "W4", "A3", "B2", "XZ", "W5", "A4",
        "B3", "A5", "B4", "P1", "B5", "SC", "WC", "OB", "X1", "RN", "P2", "P3",
        "ON", "KE", "Y1", "KV", "X2", "X3", "KX", "AT", "D1", "DZ", "Y2", "D2",
        "Y3", "D3",
    ),
    (1, False): (
        "R0", "SW", "Z1", "R1", "R2", "Z2", "SO", "SC", "W0", "W1", "A0", "W2",
        "A1", "B0", "OWN", "W3", "A2", "B1", "W4", "A3", "B2", "XZ", "W5", "A4",
        "B3", "A5", "B4", "P1", "B5", "P2", "WC", "OB", "Z3", "KE", "Y1", "X2",
        "RN", "P3", "ON", "X1", "KV", "X3", "KX", "AT", "D1", "DZ", "Y2", "D2",
        "Y3", "D3",
    ),
    (1, True): (
        "SW", "SO", "OWN", "W0", "W1", "A0", "W2", "A1", "B0", "W3", "A2", "B1",
        "W4", "A3", "B2", "XZ", "W5", "A4", "B3", "Z1", "R0", "R1", "R2", "Z2",
        "Z3", "A5", "B4", "P1", "B5", "SC", "WC", "OB", "X1", "RN", "P2", "P3",
        "ON", "KE", "Y1", "KV", "X2", "X3", "KX", "AT", "D1", "DZ", "Y2", "D2",
        "Y3", "D3",
    ),
}


def chunk_of(width, limit):
    best = 128
    for c in range(128, limit + 1, 128):
        if width % c == 0:
            best = c
    return best


def flat(v):
    shape = (v.shape[0] * v.shape[1], v.shape[2])
    if v.shape[1] % 16 == 0:
        return v.reshape(shape)
    return v.astype(F32).reshape(shape).astype(v.dtype)


def kernel(
    T, S, N, S2, NC, RC,
    lengths, tokens, wq_hbm, wkv_hbm, cache_hbm, oproj_hbm,
    ig_hbm, pg_hbm, qgain, kgain, freq,
    out_ref,
    igs, pgs, igain, pgain, cos_t, sin_t, xbuf, nbuf, w, cbuf, og, q_all, kv_all, q_snd, kv_snd, hsnd, ho, proj, inv_s, obuf,
    lsem, osem, s_w, s_x, s_c, s_o, s_oz, s_kvx, s_kv, s_q, s_h,
    r_x, r_c, r_own, r_w, r_wc, r_o, r_oc, r_q, r_kv, r_kvx, r_h,
):
    t, s, z = lax.axis_index("tmpl"), lax.axis_index("seq"), lax.axis_index("tp")
    h = N // 2
    p, b = z // h, z % h
    op = 1 - p
    zp = (z + h) % N
    R, D = tokens.shape
    HW = wq_hbm.shape[1]
    C = cache_hbm.shape[0]
    DE = D // (T * S2)
    DN = DE // NC
    RR = R // RC
    OR = oproj_hbm.shape[0] // T
    DC = oproj_hbm.shape[1]
    tc = t + 1 - 2 * (t % 2)
    par = t % 2
    ys = [(t + 2 * k) % T for k in range(1, T // 2)]
    xs = [(s + k) % S for k in range(1, S)]
    sg, sb = (s // S2) * S2, s % S2
    x2 = [(sb + k) % S2 for k in range(1, S2)]
    zs = [(z + k) % N for k in range(1, N)]

    def copy(src, dst, ssem, rsem, dev):
        return pltpu.make_async_remote_copy(
            src_ref=src, dst_ref=dst, send_sem=ssem, recv_sem=rsem,
            device_id=dev, device_id_type=MESH,
        )

    def send(src, dst, ssem, rsem, dev):
        copy(src, dst, ssem, rsem, dev).start()

    def arrived(dst, rsem):
        copy(dst, dst, s_q, rsem, {"tp": zp}).wait_recv()

    def left(src, ssem):
        copy(src, src, ssem, r_q, {"tp": zp}).wait_send()

    loc = [
        pltpu.make_async_copy(tokens, xbuf.at[b], lsem.at[0]),
        pltpu.make_async_copy(wq_hbm, w.at[0, :, pl.ds(0, HW)], lsem.at[1]),
        pltpu.make_async_copy(wkv_hbm, w.at[0, :, pl.ds(HW, 2 * HW)], lsem.at[2]),
        pltpu.make_async_copy(ig_hbm, igs, lsem.at[3]),
        pltpu.make_async_copy(pg_hbm, pgs, lsem.at[4]),
        pltpu.make_async_copy(cache_hbm, cbuf.at[s], lsem.at[5]),
    ]

    def slab(ks, kt, n):
        return (ks * T + kt) * N + n

    def slot_of(ks, kt, n):
        return (ks * (T // 2) + kt // 2) * N + n

    for k in range(T):
        loc.append(
            pltpu.make_async_copy(
                oproj_hbm.at[pl.ds(k * OR, OR)], og.at[slab(s, k, z)], lsem.at[6]
            )
        )
    for c in loc:
        c.start()

    barrier = pltpu.get_barrier_semaphore()
    peers = (
        [{"tp": k} for k in zs] + [{"seq": k} for k in xs]
        + [{"tmpl": k} for k in ys] + [{"tmpl": tc}]
    )
    for dev in peers:
        pl.semaphore_signal(barrier, inc=1, device_id=dev, device_id_type=MESH)
    pl.semaphore_wait(barrier, len(peers))

    def piece(e_t, e_s, c):
        return pl.ds(pl.multiple_of((e_t * S2 + e_s) * DE + c * DN, DN), DN)

    def send_w():
        for c in range(NC):
            pc = piece(t, sb, c)
            for src, at in ((wq_hbm, pl.ds(0, HW)), (wkv_hbm, pl.ds(HW, 2 * HW))):
                send(src.at[pc], w.at[1, pc, at], s_w, r_own.at[c], {"tp": zp})

    def send_rows(c):
        rows = pl.ds(c * RR, RR)
        for k in range(1, h):
            send(tokens.at[rows], xbuf.at[b, rows], s_x, r_x.at[b, c], {"tp": p * h + (b + k) % h})

    pt = jnp.where(z < h, jnp.where(z == h - 1, h, h - 1), jnp.where(z == h, h - 1, h))

    def o_copy(ks, kt, n, dev):
        i = slab(ks, kt, n)
        if "tmpl" in dev and dev["tmpl"] is tc:
            sem = r_oc.at[jnp.where((n == z) | (n == pt), 0, 1)]
        else:
            sem = r_o.at[slot_of(ks, kt, n)]
        send(og.at[i], og.at[i], s_o, sem, dev)

    def o_got(ks, kt, n):
        arrived(og.at[slab(ks, kt, n)], r_o.at[slot_of(ks, kt, n)])

    def z_out(n):
        rows = pl.ds(pl.multiple_of(t * OR, OR), OR)
        send(oproj_hbm.at[rows], og.at[slab(s, t, z)], s_oz, r_o.at[slot_of(s, t, z)], {"tp": n})

    def z_to(d):
        @pl.when(z + d < N)
        def _():
            z_out(jnp.minimum(z + d, N - 1))

        @pl.when(z - d >= 0)
        def _():
            z_out(jnp.maximum(z - d, 0))

    mid = (z == h - 1) | (z == h)
    lens = [lengths[k] for k in range(S)]
    offs = []
    total = jnp.int32(0)
    for k in range(S):
        offs.append(total)
        total = total + lens[k]
    own_off = jnp.int32(0)
    own_len = jnp.int32(0)
    for k in range(S):
        own_off = own_off + jnp.where(s == k, offs[k], 0)
        own_len = own_len + jnp.where(s == k, lens[k], 0)

    RB = 16 if RR % 16 == 0 else 8
    KC = chunk_of(D, 1024)

    def norm_rows(slot, first, count):
        def body(i, carry):
            rows = pl.ds(pl.multiple_of(first + i * RB, RB), RB)
            v = xbuf[slot, rows, :].astype(F32)
            inv = lax.rsqrt(jnp.sum(v * v, axis=1, keepdims=True) * (1.0 / D) + EPSILON)
            nbuf[slot, rows, :] = (v * inv * igain[...]).astype(BF16)
            return carry

        lax.fori_loop(0, count // RB, body, 0)

    def head_norm(v, gain):
        inv = lax.rsqrt(jnp.mean(v * v, axis=1, keepdims=True) + EPSILON)
        return v * inv * gain

    def project(slot, j):
        def body(i, acc):
            ks = pl.ds(pl.multiple_of(i * KC, KC), KC)
            return acc + jnp.dot(nbuf[slot, :, ks], w[j, ks, :], preferred_element_type=F32)

        v = lax.fori_loop(0, D // KC, body, jnp.zeros((R, 3 * HW), F32))
        co, si = cos_t[slot], sin_t[slot]

        def rope(u):
            return u * co + pltpu.roll(u, HW // 2, 1) * si

        q = (rope(head_norm(v[:, :HW], qgain[...])) * QUERY_SCALE).astype(BF16)
        k = rope(head_norm(v[:, HW : 2 * HW], kgain[...])).astype(BF16)
        return q, jnp.concatenate([k, v[:, 2 * HW :].astype(BF16)], axis=1)

    def share(n):
        for k in xs:
            send(kv_all.at[s, n], kv_all.at[s, n], s_kvx, r_kvx.at[s], {"seq": k})

    def own_head(slot):
        q, kv = project(slot, 0)
        n = p * h + slot
        q_all[n] = q
        kv_all[s, n] = kv
        share(n)

    def other_head(slot, late=1):
        q, kv = project(slot, 1)
        n = p * h + slot
        q_snd[slot] = q
        kv_snd[slot] = kv
        send(kv_snd.at[slot], kv_all.at[s, n], s_kv, r_kv.at[late], {"tp": zp})
        send(q_snd.at[slot], q_all.at[n], s_q, r_q, {"tp": zp})

    def tables():
        loc[3].wait()
        loc[4].wait()
        for k in range(D // 128):
            igain[0:1, k * 128 : (k + 1) * 128] = igs[k : k + 1, :]
            pgain[0:1, k * 128 : (k + 1) * 128] = pgs[k : k + 1, :]
        lane = lax.broadcasted_iota(jnp.int32, (R, HW), 1)
        for k in range(h):
            row = lax.broadcasted_iota(jnp.int32, (R, HW), 0)
            angle = (PREFIX + own_off + (p * h + k) * R + row).astype(F32) * freq[...]
            cos_t[k] = jnp.cos(angle)
            sine = jnp.sin(angle)
            sin_t[k] = jnp.where(lane < HW // 2, -sine, sine)
        loc[0].wait()
        norm_rows(b, 0, R)
        loc[1].wait()
        loc[2].wait()
        own_head(b)
        pltpu.make_async_copy(og.at[pl.ds(0, T)], og.at[pl.ds(0, T)], lsem.at[6]).wait()
    def plane(n):
        o_got(s, t, n)
        for k in xs:
            o_copy(s, t, n, {"seq": k})
        for k in ys:
            o_copy(s, t, n, {"tmpl": k})
        o_copy(s, t, n, {"tmpl": tc})

    def each(d, fn):
        @pl.when(z + d < N)
        def _():
            fn(z + d)

        @pl.when(z - d >= 0)
        def _():
            fn(z - d)

    def from_x(n, diag=True):
        for ks in xs:
            o_got(ks, t, n)
            if diag:
                for k in ys:
                    o_copy(ks, t, n, {"tmpl": k})
            o_copy(ks, t, n, {"tmpl": tc})

    def from_y(n, diag=False):
        for kt in ys:
            o_got(s, kt, n)
            if diag:
                for k in xs:
                    o_copy(s, kt, n, {"seq": k})
            o_copy(s, kt, n, {"tmpl": tc})

    def from_diag(n):
        for kt in ys:
            for ks in xs:
                o_got(ks, kt, n)
                o_copy(ks, kt, n, {"tmpl": tc})

    def w_send(e_t, e_s, c, dev):
        pc = piece(e_t, e_s, c)
        sem = r_wc if "tmpl" in dev and dev["tmpl"] is tc else r_w.at[e_t // 2, e_s, c]
        send(w.at[1, pc], w.at[1, pc], s_w, sem, dev)

    def w_own(c):
        arrived(w.at[1, piece(t, sb, c)], r_own.at[c])
        for k in x2:
            w_send(t, sb, c, {"seq": sg + k})
        for k in ys:
            w_send(t, sb, c, {"tmpl": k})
        w_send(t, sb, c, {"tmpl": tc})

    def w_got(e_t, e_s, c):
        arrived(w.at[1, piece(e_t, e_s, c)], r_w.at[e_t // 2, e_s, c])

    def w_one(c):
        for k2 in x2:
            w_got(t, k2, c)
            if c % 2 == 0:
                for k in ys:
                    w_send(t, k2, c, {"tmpl": k})
            w_send(t, k2, c, {"tmpl": tc})
        for kt in ys:
            w_got(kt, sb, c)
            if c % 2 == 1:
                for k in x2:
                    w_send(kt, sb, c, {"seq": sg + k})
            w_send(kt, sb, c, {"tmpl": tc})

    def w_two(c):
        for kt in ys:
            for k2 in x2:
                w_got(kt, k2, c)
                w_send(kt, k2, c, {"tmpl": tc})

    def take_rows(slot):
        for c in range(RC):
            rows = pl.ds(c * RR, RR)
            arrived(xbuf.at[slot, rows], r_x.at[slot, c])
            norm_rows(slot, c * RR, RR)

    def w_cross():
        arrived(w.at[1, pl.ds(0, D // 2)], r_wc)

    def send_cache():
        for k in xs:
            send(cache_hbm, cbuf.at[s], s_c, r_c.at[s], {"seq": k})

    def send_own():
        rows = pl.ds(pl.multiple_of(t * OR, OR), OR)
        i = slab(s, t, z)
        for k in xs:
            send(oproj_hbm.at[rows], og.at[i], s_o, r_o.at[slot_of(s, t, z)], {"seq": k})

    def other_rows():
        for k in range(1, h):
            take_rows((b + k) % h)
            other_head((b + k) % h)

    def own_rows():
        for k in range(1, h):
            own_head((b + k) % h)

    def wait_early():
        n = op * h + b
        arrived(kv_all.at[s, n], r_kv.at[0])
        share(n)

    def wait_kv():
        arrived(kv_all.at[s, pl.ds(op * h, h - 1)], r_kv.at[1])
        for k in range(1, h):
            share(op * h + (b + k) % h)
        arrived(q_all.at[pl.ds(op * h, h)], r_q)

    def wait_kvx():
        loc[5].wait()
        for k in xs:
            arrived(cbuf.at[k], r_c.at[k])
            arrived(kv_all.at[k], r_kvx.at[k])

    def attend(d, carry):
        m = lax.rem(z // 2 + d, h)
        q = flat(q_all[pl.ds(2 * m, 2)])
        slot_c = 2 * m * R + lax.broadcasted_iota(jnp.int32, (2 * R, 1), 0)
        pos = PREFIX + own_off + slot_c
        scores, values = [], []
        for k in range(S):
            cb = cbuf[k]
            sc = lax.dot_general(
                q, cb[:, :HW], (((1,), (1,)), ((), ())), preferred_element_type=F32
            )
            kp = PREFIX - WIN + k * C + lax.broadcasted_iota(jnp.int32, (1, C), 1)
            scores.append(jnp.where(kp > pos - WIN, sc, MASKED))
            values.append(cb[:, HW:])
            kv = flat(kv_all[k])
            sc = lax.dot_general(
                q, kv[:, :HW], (((1,), (1,)), ((), ())), preferred_element_type=F32
            )
            j = lax.broadcasted_iota(jnp.int32, (1, N * R), 1)
            kp = PREFIX + offs[k] + j
            kp = jnp.where(j < lens[k], kp, PREFIX + WIN + S * N * R)
            ok = kp <= pos
            if S * N * R > WIN:
                ok = ok & (kp > pos - WIN)
            scores.append(jnp.where(ok, sc, MASKED))
            values.append(kv[:, HW:])
        top = functools.reduce(
            jnp.maximum, [jnp.max(v, axis=1, keepdims=True) for v in scores]
        )
        row_sum = jnp.zeros((2 * R, 1), F32)
        acc = jnp.zeros((2 * R, HW), F32)
        for sc, vv in zip(scores, values):
            wt = jnp.exp(sc - top)
            row_sum = row_sum + jnp.sum(wt, axis=1, keepdims=True)
            acc = acc + jnp.dot(wt.astype(BF16), vv, preferred_element_type=F32)
        live = slot_c < own_len
        res = acc / jnp.where(live, row_sum, 1.0)
        res = jnp.where(live, res, 0.0).astype(BF16)
        for j in range(2):
            hsnd[2 * m + j] = res[j * R : (j + 1) * R]
        for j in range(2):
            n = 2 * m + j

            @pl.when(n != z)
            def _():
                send(hsnd.at[n], ho.at[z], s_h, r_h.at[z], {"tp": n})

        return carry

    def attention():
        lax.fori_loop(1, h + 1, attend, 0)
        ho[z] = hsnd[z]

    def dist(k):
        return [d for d in range(1, N) if d == k or (k == 3 and d > 3)]

    ops = {
        "SW": send_w, "OWN": tables, "SC": send_cache, "SO": send_own, "WC": w_cross,
        "OB": lambda: other_head(b, 0), "KE": wait_early, "RN": other_rows, "ON": own_rows, "KV": wait_kv,
        "KX": wait_kvx, "AT": attention, "XZ": lambda: from_x(z), "DZ": lambda: from_diag(z),
    }

    def step(tok, via=()):
        if tok in ops:
            return ops[tok]()
        kind, k = tok[0], int(tok[1])
        if kind in "WAB":
            if k < NC:
                (w_own if kind == "W" else w_one if kind == "A" else w_two)(k)
        elif kind == "R":
            if k < RC:
                send_rows(k)
        else:
            via_x = k in via
            for d in dist(k):
                if kind == "Z":
                    z_to(d)
                elif kind == "P":
                    each(d, plane)
                elif kind == "X":
                    each(d, lambda n: from_x(n, not via_x))
                elif kind == "Y":
                    each(d, lambda n: from_y(n, via_x))
                elif kind == "D":
                    each(d, from_diag)

    kinds = [(0, False), (0, True), (1, False), (1, True)]
    plans = [PLANS[k] for k in kinds]
    first = 0
    while all(len(q) > first and q[first] == plans[0][first] for q in plans):
        step(plans[0][first], VIA_X[kinds[0]])
        first += 1
    last = 0
    while all(len(q) > first + last and q[-1 - last] == plans[0][-1 - last] for q in plans):
        last += 1
    for (kp, km), q in zip(kinds, plans):
        if len(q) > first + last:
            @pl.when((par == kp) & (mid == km))
            def _():
                for tok in q[first : len(q) - last]:
                    step(tok, VIA_X[kp, km])
    for tok in plans[0][len(plans[0]) - last :]:
        step(tok, VIA_X[kinds[0]])
    CC = chunk_of(DC, 1024)
    lo, hi = jnp.minimum(z, pt), jnp.maximum(z, pt)
    rest = []
    for j in range(N - 2):
        n = j + jnp.where(j >= lo, 1, 0)
        rest.append(n + jnp.where(n >= hi, 1, 0))

    def project_out(pair, more, last=False):
        total = jnp.zeros((R, 128), F32)
        hv = jnp.concatenate([ho[n] for n in pair], axis=1)
        for k in range(S):
            def cols(i, carry):
                cs = pl.ds(pl.multiple_of(i * CC, CC), CC)
                at = pl.ds(pl.multiple_of(k * DC + i * CC, 128), CC)
                wt = jnp.concatenate(
                    [og[slab(k, kt, n), :, cs] for n in pair for kt in range(T)], axis=0
                )
                v = jnp.dot(hv, wt, preferred_element_type=F32)
                if more:
                    v = proj[:, at] + v
                proj[:, at] = v
                if last:
                    for j in range(0, CC, 128):
                        carry = carry + v[:, j : j + 128] * v[:, j : j + 128]
                return carry

            total = lax.fori_loop(0, DC // CC, cols, total)
        return total

    X, Y = S - 1, T // 2 - 1
    near = (X + S) * (T // 2)
    arrived(og.at[pl.ds(0, near)], r_oc.at[0])
    arrived(ho.at[pt], r_h.at[pt])
    project_out([z, pt], False)
    arrived(og.at[pl.ds(0, (N - 2) * S * (T // 2))], r_oc.at[1])
    for n in rest:
        arrived(ho.at[n], r_h.at[n])
    for j in range(0, N - 2, 2):
        total = project_out(rest[j : j + 2], True, j + 2 >= N - 2)
    mean = jnp.sum(total, axis=1, keepdims=True) * (1.0 / D)
    inv_s[...] = jnp.broadcast_to(lax.rsqrt(mean + EPSILON), (R, 128))

    RF = 16 if R % 16 == 0 else 8

    def finish(i, carry):
        rows = pl.ds(pl.multiple_of(i * RF, RF), RF)
        v = proj[rows, :]
        inv = inv_s[rows, :][:, :1]
        obuf[rows, :] = (xbuf[b, rows, :].astype(F32) + v * inv * pgain[...]).astype(BF16)
        pltpu.make_async_copy(obuf.at[rows], out_ref.at[rows], osem).start()
        return carry

    lax.fori_loop(0, R // RF, finish, 0)

    pltpu.make_async_copy(obuf, out_ref, osem).wait()
    left(w.at[1], s_w)
    left(xbuf.at[pl.ds(0, h - 1)], s_x)
    left(cbuf.at[pl.ds(0, S - 1)], s_c)
    left(kv_all.at[pl.ds(0, S - 1)], s_kvx)
    left(kv_snd, s_kv)
    left(q_snd, s_q)
    left(hsnd.at[pl.ds(0, N - 1)], s_h)
    count = (N - 1) * (X + Y + 1 + X * (Y + 1) + Y * S) + (Y + 1) * X * 2
    while count > 0:
        part = min(count, S * T * N)
        left(og.at[pl.ds(0, part)], s_o)
        count -= part
    left(og.at[pl.ds(0, N - 1)], s_oz)


def shards(
    T, S, N,
    tokens, lengths, input_gain, query_proj, key_value, query_gain, key_gain,
    window_cache, output_proj, post_gain,
):
    R, D = tokens.shape
    HW = query_proj.shape[1]
    C = window_cache.shape[0]
    h = N // 2
    S2 = max(d for d in range(1, S + 1) if S % d == 0 and D % (16 * T * d) == 0)
    NC = max(d for d in (1, 2, 3, 6) if D // (T * S2) % (16 * d) == 0)
    RC = 3 if R % 48 == 0 else 1
    inv = np.power(ROPE_BASE, -2.0 * np.arange(HW // 2) / HW)
    freq = np.concatenate([inv, inv])[None, :].astype(np.float32)
    OR, DC = output_proj.shape[0] // T, output_proj.shape[1]
    vm = pl.BlockSpec(memory_space=pltpu.VMEM)
    hb = pl.BlockSpec(memory_space=pltpu.HBM)
    dma = pltpu.SemaphoreType.DMA
    return pl.pallas_call(
        functools.partial(kernel, T, S, N, S2, NC, RC),
        out_shape=jax.ShapeDtypeStruct((R, D), BF16),
        in_specs=[pl.BlockSpec(memory_space=pltpu.SMEM), hb, hb, hb, hb, hb]
        + [hb, hb, vm, vm, vm],
        out_specs=hb,
        scratch_shapes=[
            pltpu.VMEM((D // 128, 128), F32),
            pltpu.VMEM((D // 128, 128), F32),
            pltpu.VMEM((1, D), F32),
            pltpu.VMEM((1, D), F32),
            pltpu.VMEM((h, R, HW), F32),
            pltpu.VMEM((h, R, HW), F32),
            pltpu.VMEM((h, R, D), BF16),
            pltpu.VMEM((h, R, D), BF16),
            pltpu.VMEM((2, D, 3 * HW), BF16),
            pltpu.VMEM((S, C, 2 * HW), BF16),
            pltpu.VMEM((S * T * N, OR, DC), BF16),
            pltpu.VMEM((N, R, HW), BF16),
            pltpu.VMEM((S, N, R, 2 * HW), BF16),
            pltpu.VMEM((h, R, HW), BF16),
            pltpu.VMEM((h, R, 2 * HW), BF16),
            pltpu.VMEM((N, R, HW), BF16),
            pltpu.VMEM((N, R, HW), BF16),
            pltpu.VMEM((R, D), F32),
            pltpu.VMEM((R, 128), F32),
            pltpu.VMEM((R, D), BF16),
            dma((7,)), dma, dma, dma, dma, dma, dma, dma, dma, dma, dma,
            dma((h, RC)), dma((S,)), dma((NC,)), dma((T // 2, S2, NC)), dma, dma((S * T // 2 * N,)), dma((2,)),
            dma, dma((2,)), dma((S,)), dma((N,)),
        ],
        compiler_params=pltpu.CompilerParams(
            collective_id=0, has_side_effects=True, vmem_limit_bytes=67043328 - R * D * 2
        ),
    )(
        lengths, tokens, query_proj, key_value, window_cache, output_proj,
        input_gain.reshape(D // 128, 128), post_gain.reshape(D // 128, 128),
        query_gain[None, :], key_gain[None, :], jnp.asarray(freq),
    )


def solution(mesh):
    T, S, N = mesh.shape["tmpl"], mesh.shape["seq"], mesh.shape["tp"]
    return jax.shard_map(
        functools.partial(shards, T, S, N),
        mesh=mesh,
        in_specs=(
            P(("tmpl", "seq", "tp"), None),
            P("tmpl"),
            P(),
            P(None, "tp"),
            P(None, "tp"),
            P(),
            P(),
            P(("tmpl", "seq"), "tp"),
            P("tp", "seq"),
            P(),
        ),
        out_specs=P(("tmpl", "seq", "tp"), None),
        check_vma=False,
    )
```

```python
import functools

import jax
import jax.numpy as jnp
import numpy as np
from jax import lax
from jax.experimental import pallas as pl
from jax.experimental.pallas import tpu as pltpu
from jax.sharding import PartitionSpec as P

WIN = 1024
PREFIX = 32768
EPSILON = 1e-06
ROPE_BASE = 10000.0
QUERY_SCALE = 168.0 ** (-0.5)
MASKED = -1e30
F32 = jnp.float32
BF16 = jnp.bfloat16
MESH = pl.DeviceIdType.MESH


VIA_X = {(0, False): (), (0, True): (), (1, False): (1,), (1, True): ()}
PLANS = {
    (0, False): (
        "SW", "Z1", "R0", "R1", "Z2", "R2", "Z3", "SO", "SC", "W0", "OWN", "W1",
        "A0", "W2", "A1", "B0", "W3", "A2", "B1", "W4", "A3", "B2", "XZ", "W5",
        "A4", "B3", "A5", "B4", "P1", "B5", "P2", "WC", "OB", "RN", "X1", "ON",
        "KE", "X2", "P3", "Y1", "KV", "X3", "KX", "AT", "D1", "DZ", "Y2", "D2",
        "Y3", "D3",
    ),
    (0, True): (
        "SW", "R0", "R1", "R2", "Z1", "Z2", "Z3", "SO", "OWN", "W0", "W1", "A0",
        "W2", "A1", "B0", "W3", "A2", "B1", "W4", "A3", "B2", "XZ", "W5", "A4",
        "B3", "A5", "B4", "P1", "B5", "SC", "WC", "OB", "X1", "RN", "P2", "P3",
        "ON", "KE", "Y1", "KV", "X2", "X3", "KX", "AT", "D1", "DZ", "Y2", "D2",
        "Y3", "D3",
    ),
    (1, False): (
        "R0", "SW", "Z1", "R1", "R2", "Z2", "SO", "SC", "W0", "W1", "A0", "W2",
        "A1", "B0", "OWN", "W3", "A2", "B1", "W4", "A3", "B2", "XZ", "W5", "A4",
        "B3", "A5", "B4", "P1", "B5", "P2", "WC", "OB", "Z3", "KE", "Y1", "X2",
        "RN", "P3", "ON", "X1", "KV", "X3", "KX", "AT", "D1", "DZ", "Y2", "D2",
        "Y3", "D3",
    ),
    (1, True): (
        "SW", "SO", "OWN", "W0", "W1", "A0", "W2", "A1", "B0", "W3", "A2", "B1",
        "W4", "A3", "B2", "XZ", "W5", "A4", "B3", "Z1", "R0", "R1", "R2", "Z2",
        "Z3", "A5", "B4", "P1", "B5", "SC", "WC", "OB", "X1", "RN", "P2", "P3",
        "ON", "KE", "Y1", "KV", "X2", "X3", "KX", "AT", "D1", "DZ", "Y2", "D2",
        "Y3", "D3",
    ),
}


def chunk_of(width, limit):
    best = 128
    for c in range(128, limit + 1, 128):
        if width % c == 0:
            best = c
    return best


def flat(v):
    shape = (v.shape[0] * v.shape[1], v.shape[2])
    if v.shape[1] % 16 == 0:
        return v.reshape(shape)
    return v.astype(F32).reshape(shape).astype(v.dtype)


def kernel(
    T, S, N, S2, NC, RC,
    lengths, tokens, wq_hbm, wkv_hbm, cache_hbm, oproj_hbm,
    ig_hbm, pg_hbm, qgain, kgain, freq,
    out_ref,
    igs, pgs, igain, pgain, cos_t, sin_t, xbuf, nbuf, w, cbuf, og, q_all, kv_all, q_snd, kv_snd, hsnd, ho, proj, inv_s, obuf,
    lsem, osem, s_w, s_x, s_c, s_o, s_oz, s_kvx, s_kv, s_q, s_h,
    r_x, r_c, r_own, r_w, r_wc, r_o, r_oc, r_q, r_kv, r_kvx, r_h,
):
    t, s, z = lax.axis_index("tmpl"), lax.axis_index("seq"), lax.axis_index("tp")
    h = N // 2
    p, b = z // h, z % h
    op = 1 - p
    zp = (z + h) % N
    R, D = tokens.shape
    HW = wq_hbm.shape[1]
    C = cache_hbm.shape[0]
    DE = D // (T * S2)
    DN = DE // NC
    RR = R // RC
    OR = oproj_hbm.shape[0] // T
    DC = oproj_hbm.shape[1]
    tc = t + 1 - 2 * (t % 2)
    par = t % 2
    ys = [(t + 2 * k) % T for k in range(1, T // 2)]
    xs = [(s + k) % S for k in range(1, S)]
    sg, sb = (s // S2) * S2, s % S2
    x2 = [(sb + k) % S2 for k in range(1, S2)]
    zs = [(z + k) % N for k in range(1, N)]

    def copy(src, dst, ssem, rsem, dev):
        return pltpu.make_async_remote_copy(
            src_ref=src, dst_ref=dst, send_sem=ssem, recv_sem=rsem,
            device_id=dev, device_id_type=MESH,
        )

    def send(src, dst, ssem, rsem, dev):
        copy(src, dst, ssem, rsem, dev).start()

    def arrived(dst, rsem):
        copy(dst, dst, s_q, rsem, {"tp": zp}).wait_recv()

    def left(src, ssem):
        copy(src, src, ssem, r_q, {"tp": zp}).wait_send()

    loc = [
        pltpu.make_async_copy(tokens, xbuf.at[b], lsem.at[0]),
        pltpu.make_async_copy(wq_hbm, w.at[0, :, pl.ds(0, HW)], lsem.at[1]),
        pltpu.make_async_copy(wkv_hbm, w.at[0, :, pl.ds(HW, 2 * HW)], lsem.at[2]),
        pltpu.make_async_copy(ig_hbm, igs, lsem.at[3]),
        pltpu.make_async_copy(pg_hbm, pgs, lsem.at[4]),
        pltpu.make_async_copy(cache_hbm, cbuf.at[s], lsem.at[5]),
    ]

    def slab(ks, kt, n):
        return (ks * T + kt) * N + n

    def slot_of(ks, kt, n):
        return (ks * (T // 2) + kt // 2) * N + n

    for k in range(T):
        loc.append(
            pltpu.make_async_copy(
                oproj_hbm.at[pl.ds(k * OR, OR)], og.at[slab(s, k, z)], lsem.at[6]
            )
        )
    for c in loc:
        c.start()

    barrier = pltpu.get_barrier_semaphore()
    peers = (
        [{"tp": k} for k in zs] + [{"seq": k} for k in xs]
        + [{"tmpl": k} for k in ys] + [{"tmpl": tc}]
    )
    for dev in peers:
        pl.semaphore_signal(barrier, inc=1, device_id=dev, device_id_type=MESH)
    pl.semaphore_wait(barrier, len(peers))

    def piece(e_t, e_s, c):
        return pl.ds(pl.multiple_of((e_t * S2 + e_s) * DE + c * DN, DN), DN)

    def send_w():
        for c in range(NC):
            pc = piece(t, sb, c)
            for src, at in ((wq_hbm, pl.ds(0, HW)), (wkv_hbm, pl.ds(HW, 2 * HW))):
                send(src.at[pc], w.at[1, pc, at], s_w, r_own.at[c], {"tp": zp})

    def send_rows(c):
        rows = pl.ds(c * RR, RR)
        for k in range(1, h):
            send(tokens.at[rows], xbuf.at[b, rows], s_x, r_x.at[b, c], {"tp": p * h + (b + k) % h})

    pt = jnp.where(z < h, jnp.where(z == h - 1, h, h - 1), jnp.where(z == h, h - 1, h))

    def o_copy(ks, kt, n, dev):
        i = slab(ks, kt, n)
        if "tmpl" in dev and dev["tmpl"] is tc:
            sem = r_oc.at[jnp.where((n == z) | (n == pt), 0, 1)]
        else:
            sem = r_o.at[slot_of(ks, kt, n)]
        send(og.at[i], og.at[i], s_o, sem, dev)

    def o_got(ks, kt, n):
        arrived(og.at[slab(ks, kt, n)], r_o.at[slot_of(ks, kt, n)])

    def z_out(n):
        rows = pl.ds(pl.multiple_of(t * OR, OR), OR)
        send(oproj_hbm.at[rows], og.at[slab(s, t, z)], s_oz, r_o.at[slot_of(s, t, z)], {"tp": n})

    def z_to(d):
        @pl.when(z + d < N)
        def _():
            z_out(jnp.minimum(z + d, N - 1))

        @pl.when(z - d >= 0)
        def _():
            z_out(jnp.maximum(z - d, 0))

    mid = (z == h - 1) | (z == h)
    lens = [lengths[k] for k in range(S)]
    offs = []
    total = jnp.int32(0)
    for k in range(S):
        offs.append(total)
        total = total + lens[k]
    own_off = jnp.int32(0)
    own_len = jnp.int32(0)
    for k in range(S):
        own_off = own_off + jnp.where(s == k, offs[k], 0)
        own_len = own_len + jnp.where(s == k, lens[k], 0)

    RB = 16 if RR % 16 == 0 else 8
    KC = chunk_of(D, 1024)

    def norm_rows(slot, first, count):
        def body(i, carry):
            rows = pl.ds(pl.multiple_of(first + i * RB, RB), RB)
            v = xbuf[slot, rows, :].astype(F32)
            inv = lax.rsqrt(jnp.sum(v * v, axis=1, keepdims=True) * (1.0 / D) + EPSILON)
            nbuf[slot, rows, :] = (v * inv * igain[...]).astype(BF16)
            return carry

        lax.fori_loop(0, count // RB, body, 0)

    def head_norm(v, gain):
        inv = lax.rsqrt(jnp.mean(v * v, axis=1, keepdims=True) + EPSILON)
        return v * inv * gain

    def project(slot, j):
        def body(i, acc):
            ks = pl.ds(pl.multiple_of(i * KC, KC), KC)
            return acc + jnp.dot(nbuf[slot, :, ks], w[j, ks, :], preferred_element_type=F32)

        v = lax.fori_loop(0, D // KC, body, jnp.zeros((R, 3 * HW), F32))
        co, si = cos_t[slot], sin_t[slot]

        def rope(u):
            return u * co + pltpu.roll(u, HW // 2, 1) * si

        q = (rope(head_norm(v[:, :HW], qgain[...])) * QUERY_SCALE).astype(BF16)
        k = rope(head_norm(v[:, HW : 2 * HW], kgain[...])).astype(BF16)
        return q, jnp.concatenate([k, v[:, 2 * HW :].astype(BF16)], axis=1)

    def share(n):
        for k in xs:
            send(kv_all.at[s, n], kv_all.at[s, n], s_kvx, r_kvx.at[s], {"seq": k})

    def own_head(slot):
        q, kv = project(slot, 0)
        n = p * h + slot
        q_all[n] = q
        kv_all[s, n] = kv
        share(n)

    def other_head(slot, late=1):
        q, kv = project(slot, 1)
        n = p * h + slot
        q_snd[slot] = q
        kv_snd[slot] = kv
        send(kv_snd.at[slot], kv_all.at[s, n], s_kv, r_kv.at[late], {"tp": zp})
        send(q_snd.at[slot], q_all.at[n], s_q, r_q, {"tp": zp})

    def tables():
        loc[3].wait()
        loc[4].wait()
        for k in range(D // 128):
            igain[0:1, k * 128 : (k + 1) * 128] = igs[k : k + 1, :]
            pgain[0:1, k * 128 : (k + 1) * 128] = pgs[k : k + 1, :]
        lane = lax.broadcasted_iota(jnp.int32, (R, HW), 1)
        for k in range(h):
            row = lax.broadcasted_iota(jnp.int32, (R, HW), 0)
            angle = (PREFIX + own_off + (p * h + k) * R + row).astype(F32) * freq[...]
            cos_t[k] = jnp.cos(angle)
            sine = jnp.sin(angle)
            sin_t[k] = jnp.where(lane < HW // 2, -sine, sine)
        loc[0].wait()
        norm_rows(b, 0, R)
        loc[1].wait()
        loc[2].wait()
        own_head(b)
        pltpu.make_async_copy(og.at[pl.ds(0, T)], og.at[pl.ds(0, T)], lsem.at[6]).wait()
    def plane(n):
        o_got(s, t, n)
        for k in xs:
            o_copy(s, t, n, {"seq": k})
        for k in ys:
            o_copy(s, t, n, {"tmpl": k})
        o_copy(s, t, n, {"tmpl": tc})

    def each(d, fn):
        @pl.when(z + d < N)
        def _():
            fn(z + d)

        @pl.when(z - d >= 0)
        def _():
            fn(z - d)

    def from_x(n, diag=True):
        for ks in xs:
            o_got(ks, t, n)
            if diag:
                for k in ys:
                    o_copy(ks, t, n, {"tmpl": k})
            o_copy(ks, t, n, {"tmpl": tc})

    def from_y(n, diag=False):
        for kt in ys:
            o_got(s, kt, n)
            if diag:
                for k in xs:
                    o_copy(s, kt, n, {"seq": k})
            o_copy(s, kt, n, {"tmpl": tc})

    def from_diag(n):
        for kt in ys:
            for ks in xs:
                o_got(ks, kt, n)
                o_copy(ks, kt, n, {"tmpl": tc})

    def w_send(e_t, e_s, c, dev):
        pc = piece(e_t, e_s, c)
        sem = r_wc if "tmpl" in dev and dev["tmpl"] is tc else r_w.at[e_t // 2, e_s, c]
        send(w.at[1, pc], w.at[1, pc], s_w, sem, dev)

    def w_own(c):
        arrived(w.at[1, piece(t, sb, c)], r_own.at[c])
        for k in x2:
            w_send(t, sb, c, {"seq": sg + k})
        for k in ys:
            w_send(t, sb, c, {"tmpl": k})
        w_send(t, sb, c, {"tmpl": tc})

    def w_got(e_t, e_s, c):
        arrived(w.at[1, piece(e_t, e_s, c)], r_w.at[e_t // 2, e_s, c])

    def w_one(c):
        for k2 in x2:
            w_got(t, k2, c)
            if c % 2 == 0:
                for k in ys:
                    w_send(t, k2, c, {"tmpl": k})
            w_send(t, k2, c, {"tmpl": tc})
        for kt in ys:
            w_got(kt, sb, c)
            if c % 2 == 1:
                for k in x2:
                    w_send(kt, sb, c, {"seq": sg + k})
            w_send(kt, sb, c, {"tmpl": tc})

    def w_two(c):
        for kt in ys:
            for k2 in x2:
                w_got(kt, k2, c)
                w_send(kt, k2, c, {"tmpl": tc})

    def take_rows(slot):
        for c in range(RC):
            rows = pl.ds(c * RR, RR)
            arrived(xbuf.at[slot, rows], r_x.at[slot, c])
            norm_rows(slot, c * RR, RR)

    def w_cross():
        arrived(w.at[1, pl.ds(0, D // 2)], r_wc)

    def send_cache():
        for k in xs:
            send(cache_hbm, cbuf.at[s], s_c, r_c.at[s], {"seq": k})

    def send_own():
        rows = pl.ds(pl.multiple_of(t * OR, OR), OR)
        i = slab(s, t, z)
        for k in xs:
            send(oproj_hbm.at[rows], og.at[i], s_o, r_o.at[slot_of(s, t, z)], {"seq": k})

    def other_rows():
        for k in range(1, h):
            take_rows((b + k) % h)
            other_head((b + k) % h)

    def own_rows():
        for k in range(1, h):
            own_head((b + k) % h)

    def wait_early():
        n = op * h + b
        arrived(kv_all.at[s, n], r_kv.at[0])
        share(n)

    def wait_kv():
        arrived(kv_all.at[s, pl.ds(op * h, h - 1)], r_kv.at[1])
        for k in range(1, h):
            share(op * h + (b + k) % h)
        arrived(q_all.at[pl.ds(op * h, h)], r_q)

    def wait_kvx():
        loc[5].wait()
        for k in xs:
            arrived(cbuf.at[k], r_c.at[k])
            arrived(kv_all.at[k], r_kvx.at[k])

    def attend(d, carry):
        m = lax.rem(z // 2 + d, h)
        q = flat(q_all[pl.ds(2 * m, 2)])
        slot_c = 2 * m * R + lax.broadcasted_iota(jnp.int32, (2 * R, 1), 0)
        pos = PREFIX + own_off + slot_c
        scores, values = [], []
        for k in range(S):
            cb = cbuf[k]
            sc = lax.dot_general(
                q, cb[:, :HW], (((1,), (1,)), ((), ())), preferred_element_type=F32
            )
            kp = PREFIX - WIN + k * C + lax.broadcasted_iota(jnp.int32, (1, C), 1)
            scores.append(jnp.where(kp > pos - WIN, sc, MASKED))
            values.append(cb[:, HW:])
            kv = flat(kv_all[k])
            sc = lax.dot_general(
                q, kv[:, :HW], (((1,), (1,)), ((), ())), preferred_element_type=F32
            )
            j = lax.broadcasted_iota(jnp.int32, (1, N * R), 1)
            kp = PREFIX + offs[k] + j
            kp = jnp.where(j < lens[k], kp, PREFIX + WIN + S * N * R)
            ok = kp <= pos
            if S * N * R > WIN:
                ok = ok & (kp > pos - WIN)
            scores.append(jnp.where(ok, sc, MASKED))
            values.append(kv[:, HW:])
        top = functools.reduce(
            jnp.maximum, [jnp.max(v, axis=1, keepdims=True) for v in scores]
        )
        row_sum = jnp.zeros((2 * R, 1), F32)
        acc = jnp.zeros((2 * R, HW), F32)
        for sc, vv in zip(scores, values):
            wt = jnp.exp(sc - top)
            row_sum = row_sum + jnp.sum(wt, axis=1, keepdims=True)
            acc = acc + jnp.dot(wt.astype(BF16), vv, preferred_element_type=F32)
        live = slot_c < own_len
        res = acc / jnp.where(live, row_sum, 1.0)
        res = jnp.where(live, res, 0.0).astype(BF16)
        for j in range(2):
            hsnd[2 * m + j] = res[j * R : (j + 1) * R]
        for j in range(2):
            n = 2 * m + j

            @pl.when(n != z)
            def _():
                send(hsnd.at[n], ho.at[z], s_h, r_h.at[z], {"tp": n})

        return carry

    def attention():
        lax.fori_loop(1, h + 1, attend, 0)
        ho[z] = hsnd[z]

    def dist(k):
        return [d for d in range(1, N) if d == k or (k == 3 and d > 3)]

    ops = {
        "SW": send_w, "OWN": tables, "SC": send_cache, "SO": send_own, "WC": w_cross,
        "OB": lambda: other_head(b, 0), "KE": wait_early, "RN": other_rows, "ON": own_rows, "KV": wait_kv,
        "KX": wait_kvx, "AT": attention, "XZ": lambda: from_x(z), "DZ": lambda: from_diag(z),
    }

    def step(tok, via=()):
        if tok in ops:
            return ops[tok]()
        kind, k = tok[0], int(tok[1])
        if kind in "WAB":
            if k < NC:
                (w_own if kind == "W" else w_one if kind == "A" else w_two)(k)
        elif kind == "R":
            if k < RC:
                send_rows(k)
        else:
            via_x = k in via
            for d in dist(k):
                if kind == "Z":
                    z_to(d)
                elif kind == "P":
                    each(d, plane)
                elif kind == "X":
                    each(d, lambda n: from_x(n, not via_x))
                elif kind == "Y":
                    each(d, lambda n: from_y(n, via_x))
                elif kind == "D":
                    each(d, from_diag)

    kinds = [(0, False), (0, True), (1, False), (1, True)]
    plans = [PLANS[k] for k in kinds]
    first = 0
    while all(len(q) > first and q[first] == plans[0][first] for q in plans):
        step(plans[0][first], VIA_X[kinds[0]])
        first += 1
    last = 0
    while all(len(q) > first + last and q[-1 - last] == plans[0][-1 - last] for q in plans):
        last += 1
    for (kp, km), q in zip(kinds, plans):
        if len(q) > first + last:
            @pl.when((par == kp) & (mid == km))
            def _():
                for tok in q[first : len(q) - last]:
                    step(tok, VIA_X[kp, km])
    for tok in plans[0][len(plans[0]) - last :]:
        step(tok, VIA_X[kinds[0]])
    CC = chunk_of(DC, 2048)
    lo, hi = jnp.minimum(z, pt), jnp.maximum(z, pt)
    rest = []
    for j in range(N - 2):
        n = j + jnp.where(j >= lo, 1, 0)
        rest.append(n + jnp.where(n >= hi, 1, 0))

    def project_out(pair, more, last=False):
        total = jnp.zeros((R, 128), F32)
        hv = jnp.concatenate([ho[n] for n in pair], axis=1)
        for k in range(S):
            def cols(i, carry):
                cs = pl.ds(pl.multiple_of(i * CC, CC), CC)
                at = pl.ds(pl.multiple_of(k * DC + i * CC, 128), CC)
                wt = jnp.concatenate(
                    [og[slab(k, kt, n), :, cs] for n in pair for kt in range(T)], axis=0
                )
                v = jnp.dot(hv, wt, preferred_element_type=F32)
                if more:
                    v = proj[:, at] + v
                proj[:, at] = v
                if last:
                    for j in range(0, CC, 128):
                        carry = carry + v[:, j : j + 128] * v[:, j : j + 128]
                return carry

            total = lax.fori_loop(0, DC // CC, cols, total)
        return total

    X, Y = S - 1, T // 2 - 1
    near = (X + S) * (T // 2)
    arrived(og.at[pl.ds(0, near)], r_oc.at[0])
    arrived(ho.at[pt], r_h.at[pt])
    project_out([z, pt], False)
    arrived(og.at[pl.ds(0, (N - 2) * S * (T // 2))], r_oc.at[1])
    for n in rest:
        arrived(ho.at[n], r_h.at[n])
    for j in range(0, N - 2, 2):
        total = project_out(rest[j : j + 2], True, j + 2 >= N - 2)
    mean = jnp.sum(total, axis=1, keepdims=True) * (1.0 / D)
    inv_s[...] = jnp.broadcast_to(lax.rsqrt(mean + EPSILON), (R, 128))

    RF = 16 if R % 16 == 0 else 8

    def finish(i, carry):
        rows = pl.ds(pl.multiple_of(i * RF, RF), RF)
        v = proj[rows, :]
        inv = inv_s[rows, :][:, :1]
        obuf[rows, :] = (xbuf[b, rows, :].astype(F32) + v * inv * pgain[...]).astype(BF16)
        pltpu.make_async_copy(obuf.at[rows], out_ref.at[rows], osem).start()
        return carry

    lax.fori_loop(0, R // RF, finish, 0, unroll=True)

    pltpu.make_async_copy(obuf, out_ref, osem).wait()
    left(w.at[1], s_w)
    left(xbuf.at[pl.ds(0, h - 1)], s_x)
    left(cbuf.at[pl.ds(0, S - 1)], s_c)
    left(kv_all.at[pl.ds(0, S - 1)], s_kvx)
    left(kv_snd, s_kv)
    left(q_snd, s_q)
    left(hsnd.at[pl.ds(0, N - 1)], s_h)
    count = (N - 1) * (X + Y + 1 + X * (Y + 1) + Y * S) + (Y + 1) * X * 2
    while count > 0:
        part = min(count, S * T * N)
        left(og.at[pl.ds(0, part)], s_o)
        count -= part
    left(og.at[pl.ds(0, N - 1)], s_oz)


def shards(
    T, S, N,
    tokens, lengths, input_gain, query_proj, key_value, query_gain, key_gain,
    window_cache, output_proj, post_gain,
):
    R, D = tokens.shape
    HW = query_proj.shape[1]
    C = window_cache.shape[0]
    h = N // 2
    S2 = max(d for d in range(1, S + 1) if S % d == 0 and D % (16 * T * d) == 0)
    NC = max(d for d in (1, 2, 3, 6) if D // (T * S2) % (16 * d) == 0)
    RC = 3 if R % 48 == 0 else 1
    inv = np.power(ROPE_BASE, -2.0 * np.arange(HW // 2) / HW)
    freq = np.concatenate([inv, inv])[None, :].astype(np.float32)
    OR, DC = output_proj.shape[0] // T, output_proj.shape[1]
    vm = pl.BlockSpec(memory_space=pltpu.VMEM)
    hb = pl.BlockSpec(memory_space=pltpu.HBM)
    dma = pltpu.SemaphoreType.DMA
    return pl.pallas_call(
        functools.partial(kernel, T, S, N, S2, NC, RC),
        out_shape=jax.ShapeDtypeStruct((R, D), BF16),
        in_specs=[pl.BlockSpec(memory_space=pltpu.SMEM), hb, hb, hb, hb, hb]
        + [hb, hb, vm, vm, vm],
        out_specs=hb,
        scratch_shapes=[
            pltpu.VMEM((D // 128, 128), F32),
            pltpu.VMEM((D // 128, 128), F32),
            pltpu.VMEM((1, D), F32),
            pltpu.VMEM((1, D), F32),
            pltpu.VMEM((h, R, HW), F32),
            pltpu.VMEM((h, R, HW), F32),
            pltpu.VMEM((h, R, D), BF16),
            pltpu.VMEM((h, R, D), BF16),
            pltpu.VMEM((2, D, 3 * HW), BF16),
            pltpu.VMEM((S, C, 2 * HW), BF16),
            pltpu.VMEM((S * T * N, OR, DC), BF16),
            pltpu.VMEM((N, R, HW), BF16),
            pltpu.VMEM((S, N, R, 2 * HW), BF16),
            pltpu.VMEM((h, R, HW), BF16),
            pltpu.VMEM((h, R, 2 * HW), BF16),
            pltpu.VMEM((N, R, HW), BF16),
            pltpu.VMEM((N, R, HW), BF16),
            pltpu.VMEM((R, D), F32),
            pltpu.VMEM((R, 128), F32),
            pltpu.VMEM((R, D), BF16),
            dma((7,)), dma, dma, dma, dma, dma, dma, dma, dma, dma, dma,
            dma((h, RC)), dma((S,)), dma((NC,)), dma((T // 2, S2, NC)), dma, dma((S * T // 2 * N,)), dma((2,)),
            dma, dma((2,)), dma((S,)), dma((N,)),
        ],
        compiler_params=pltpu.CompilerParams(
            collective_id=0, has_side_effects=True, vmem_limit_bytes=67043328 - R * D * 2
        ),
    )(
        lengths, tokens, query_proj, key_value, window_cache, output_proj,
        input_gain.reshape(D // 128, 128), post_gain.reshape(D // 128, 128),
        query_gain[None, :], key_gain[None, :], jnp.asarray(freq),
    )


def solution(mesh):
    T, S, N = mesh.shape["tmpl"], mesh.shape["seq"], mesh.shape["tp"]
    return jax.shard_map(
        functools.partial(shards, T, S, N),
        mesh=mesh,
        in_specs=(
            P(("tmpl", "seq", "tp"), None),
            P("tmpl"),
            P(),
            P(None, "tp"),
            P(None, "tp"),
            P(),
            P(),
            P(("tmpl", "seq"), "tp"),
            P("tp", "seq"),
            P(),
        ),
        out_specs=P(("tmpl", "seq", "tp"), None),
        check_vma=False,
    )
```
